32 devices in a mesh: batch: 8 (over y, x, core), kv: 4 (over z).
Axes of the slice: x: 2, y: 2, z: 4, core: 2. Of those that a mesh axis runs over, the one named last changes fastest.
Arguments:
- inputs: bfloat16 [8, 1024, 1024], P('batch'), may hold values from -6 to 6
- memory: bfloat16 [8, 1024, 1024], P('batch'), may hold values from -6 to 6
- out_grad: bfloat16 [8, 1024, 1024], P('batch'), may hold values from -6 to 6
- gain_self: bfloat16 [1024], replicated, may hold values from 0.5 to 1.5
- self_query: bfloat16 [1024, 1024], P(None, 'kv'), may hold values from -0.046875 to 0.046875
- self_key: bfloat16 [1024, 512], P(None, 'kv'), may hold values from -0.1875 to 0.1875
- self_value: bfloat16 [1024, 512], P(None, 'kv'), may hold values from -0.1875 to 0.1875
- self_output: bfloat16 [1024, 1024], P('kv'), may hold values from -0.75 to 0.75
- self_table: bfloat16 [32, 16], P(None, 'kv'), may hold values from -4 to 4
- gain_cross: bfloat16 [1024], replicated, may hold values from 0.5 to 1.5
- cross_query: bfloat16 [1024, 1024], P(None, 'kv'), may hold values from -0.046875 to 0.046875
- cross_key: bfloat16 [1024, 512], P(None, 'kv'), may hold values from -0.1875 to 0.1875
- cross_value: bfloat16 [1024, 512], P(None, 'kv'), may hold values from -0.1875 to 0.1875
- cross_output: bfloat16 [1024, 1024], P('kv'), may hold values from -0.75 to 0.75
- cross_table: bfloat16 [32, 16], P(None, 'kv'), may hold values from -4 to 4
- gain_ffn: bfloat16 [1024], replicated, may hold values from 0.5 to 1.5
- ffn_gate: bfloat16 [1024, 2816], P(None, 'kv'), may hold values from -0.1875 to 0.1875
- ffn_up: bfloat16 [1024, 2816], P(None, 'kv'), may hold values from -0.1875 to 0.1875
- ffn_down: bfloat16 [2816, 1024], P('kv'), may hold values from -0.109375 to 0.109375
Outputs:
- layer_out: bfloat16 [8, 1024, 1024], P('batch')
- input_grad: float32 [8, 1024, 1024], P('batch')
- memory_grad: float32 [8, 1024, 1024], P('batch', None, 'kv')
- grad_gain_self: float32 [1024], replicated
- grad_self_query: float32 [1024, 1024], P(None, 'kv')
- grad_self_key: float32 [1024, 512], P(None, 'kv')
- grad_self_value: float32 [1024, 512], P(None, 'kv')
- grad_self_output: float32 [1024, 1024], P('kv')
- grad_self_table: float32 [32, 16], P(None, 'kv')
- grad_gain_cross: float32 [1024], replicated
- grad_cross_query: float32 [1024, 1024], P(None, 'kv')
- grad_cross_key: float32 [1024, 512], P(None, 'kv')
- grad_cross_value: float32 [1024, 512], P(None, 'kv')
- grad_cross_output: float32 [1024, 1024], P('kv')
- grad_cross_table: float32 [32, 16], P(None, 'kv')
- grad_gain_ffn: float32 [1024], replicated
- grad_ffn_gate: float32 [1024, 2816], P(None, 'kv')
- grad_ffn_up: float32 [1024, 2816], P(None, 'kv')
- grad_ffn_down: float32 [2816, 1024], P('kv')
The draws below stay inside these ranges and needn't reach their ends.
All inputs are finite; a program needn't handle non-finite values.
Results may differ from the reference program's by a relative error of at most 0.034.
The reference program's roundings to bfloat16 on the way count: a program that leaves them out, or rounds other values in their place, can miss the bound.
Values sent between devices are 32-bit elements; how exact they have to be, the bound alone decides.
No kernel may reach another device: no remote copies, remote signals or barrier semaphores. Data moves between devices by JAX's collectives and lax.ppermute only.
A program may use at most 192 MiB of HBM per device.

```python
import math
import jax
import jax.numpy as jnp
import numpy as np
from jax import lax

D = 1024
HQ = 16
DH = 64
FF = 2816
BUCKETS = 32
MAXDIST = 128
GROUPS = 8
LEN = 1024
MEM = 1024
SEQS = 8


def block_levels(stream_key, shape, split, low, largest):
    def one(dim, blocks):
        heights = jax.random.uniform(jax.random.fold_in(jax.random.fold_in(stream_key, 6), dim), (blocks,), jnp.float32, low / len(split), largest / len(split))
        return jnp.repeat(jnp.exp(heights), shape[dim] // blocks).reshape((-1,) + (1,) * (len(shape) - dim - 1))

    gain = one(*split[0])
    for cut in split[1:]:
        gain = gain * one(*cut)
    return gain


def noise(key, shape, scale, most, cuts=(), held_as=jnp.bfloat16):
    array = scale * jax.random.normal(key, shape, jnp.float32)
    if cuts:
        array = array * block_levels(key, shape, cuts, -0.22, 0.18)
    return jnp.clip(array, -most, most).astype(held_as)


def setup_inputs(seed: int = 0) -> dict:
    keys = jax.random.split(jax.random.key(seed), 20)
    return {
        "inputs": noise(keys[0], (SEQS, LEN, D), 1.0, 6.0, ((0, 8),)),
        "memory": noise(keys[1], (SEQS, MEM, D), 1.0, 6.0, ((0, 8),)),
        "out_grad": noise(keys[2], (SEQS, LEN, D), 1.0, 6.0, ((0, 8),)),
        "gain_self": jnp.clip(1.0 + 0.1 * jax.random.normal(keys[3], (D,), jnp.float32), 0.5, 1.5).astype(jnp.bfloat16),
        "self_query": noise(keys[4], (D, HQ * DH), (16 * D) ** -0.5, 0.046875, ((1, 4),)),
        "self_key": noise(keys[5], (D, GROUPS * DH), D ** -0.5, 0.1875, ((1, 4),)),
        "self_value": noise(keys[6], (D, GROUPS * DH), D ** -0.5, 0.1875, ((1, 4),)),
        "self_output": noise(keys[7], (HQ * DH, D), (HQ * DH // 16) ** -0.5, 0.75, ((0, 4),)),
        "self_table": noise(keys[8], (BUCKETS, HQ), 1.0, 4.0, ((1, 4),)),
        "gain_cross": jnp.clip(1.0 + 0.1 * jax.random.normal(keys[9], (D,), jnp.float32), 0.5, 1.5).astype(jnp.bfloat16),
        "cross_query": noise(keys[10], (D, HQ * DH), (16 * D) ** -0.5, 0.046875, ((1, 4),)),
        "cross_key": noise(keys[11], (D, GROUPS * DH), D ** -0.5, 0.1875, ((1, 4),)),
        "cross_value": noise(keys[12], (D, GROUPS * DH), D ** -0.5, 0.1875, ((1, 4),)),
        "cross_output": noise(keys[13], (HQ * DH, D), (HQ * DH // 16) ** -0.5, 0.75, ((0, 4),)),
        "cross_table": noise(keys[14], (BUCKETS, HQ), 1.0, 4.0, ((1, 4),)),
        "gain_ffn": jnp.clip(1.0 + 0.1 * jax.random.normal(keys[15], (D,), jnp.float32), 0.5, 1.5).astype(jnp.bfloat16),
        "ffn_gate": noise(keys[16], (D, FF), D ** -0.5, 0.1875, ((1, 4),)),
        "ffn_up": noise(keys[17], (D, FF), D ** -0.5, 0.1875, ((1, 4),)),
        "ffn_down": noise(keys[18], (FF, D), FF ** -0.5, 0.109375, ((0, 4),)),
    }


@jax.custom_vjp
def low(v):
    return lax.optimization_barrier(v.astype(jnp.bfloat16)).astype(jnp.float32)

@jax.custom_vjp
def low_back(v):
    return v

def low_keep(v):
    return (low(v), None)

def low_pass(kept, grad):
    return (grad,)

def back_keep(v):
    return (v, None)

def back_low(kept, grad):
    return (low(grad),)
low.defvjp(low_keep, low_pass)
low_back.defvjp(back_keep, back_low)
eps = 1e-06
masked_value = -1e+30

def bucket_ids(extent, offset, two_sided, buckets, reach):
    relative = np.arange(extent) - offset
    if two_sided:
        per_side = buckets // 2
        base_id = (relative > 0).astype(np.int64) * per_side
        distance = np.abs(relative)
    else:
        per_side = buckets
        base_id = np.zeros(extent, np.int64)
        distance = np.maximum(-relative, 0)
    exact_end = per_side // 2
    scaled = np.log(np.maximum(distance, 1) / exact_end) / math.log(reach / exact_end)
    far_id = np.minimum(exact_end + np.floor(scaled * (per_side - exact_end)).astype(np.int64), per_side - 1)
    return np.where(distance < exact_end, distance, far_id) + base_id

def offset_ids(seq_len, key_len, two_sided):
    table_ids = bucket_ids(seq_len + key_len - 1, seq_len - 1, two_sided, BUCKETS, MAXDIST)
    offsets = np.arange(key_len)[None, :] - np.arange(seq_len)[:, None] + seq_len - 1
    return jnp.asarray(table_ids[offsets], dtype=jnp.int32)

def rms_norm(hidden, gain_vec):
    inv_scale = lax.rsqrt(lax.optimization_barrier(jnp.mean(hidden * hidden, axis=-1, keepdims=True)) + eps)
    return hidden * inv_scale * gain_vec

def matmul(left_mat, right_mat):
    return jnp.dot(left_mat, right_mat, precision=lax.Precision.HIGHEST)

def attend(queries, key_rows, value_rows, bias_heads, keep_mask):
    seq_len = queries.shape[0]
    key_len = key_rows.shape[0]
    per_group = HQ // GROUPS
    grouped = queries.reshape(seq_len, GROUPS, per_group, DH)
    key_heads = key_rows.reshape(key_len, GROUPS, DH)
    value_heads = value_rows.reshape(key_len, GROUPS, DH)
    scores = jnp.einsum('qgrd,kgd->grqk', grouped, key_heads, precision=lax.Precision.HIGHEST)
    scores = low_back(scores + bias_heads.reshape(GROUPS, per_group, seq_len, key_len))
    if keep_mask is not None:
        scores = jnp.where(keep_mask, scores, masked_value)
    weights = low(jax.nn.softmax(scores, axis=-1))
    mixed_heads = jnp.einsum('grqk,kgd->qgrd', weights, value_heads, precision=lax.Precision.HIGHEST)
    return low(low_back(mixed_heads.reshape(seq_len, HQ * DH)))

def forward(inputs, memory, gain_self, self_query, self_key, self_value, self_output, self_table, gain_cross, cross_query, cross_key, cross_value, cross_output, cross_table, gain_ffn, ffn_gate, ffn_up, ffn_down):
    seq_len = inputs.shape[0]
    key_len = memory.shape[0]
    self_ids = offset_ids(seq_len, seq_len, False)
    cross_ids = offset_ids(seq_len, key_len, True)
    keep_mask = jnp.asarray(np.tril(np.ones((seq_len, seq_len), dtype=bool)))
    attn_in = low(rms_norm(inputs, gain_self))
    queries = low(low_back(matmul(attn_in, self_query)))
    key_rows = low(low_back(matmul(attn_in, self_key)))
    value_rows = low(low_back(matmul(attn_in, self_value)))
    self_bias = jnp.transpose(self_table[self_ids], (2, 0, 1))
    mixed_self = attend(queries, key_rows, value_rows, self_bias, keep_mask)
    after_self = inputs + low_back(matmul(mixed_self, self_output))
    cross_in = low(rms_norm(after_self, gain_cross))
    cross_q = low(low_back(matmul(cross_in, cross_query)))
    cross_k = low(low_back(matmul(memory, cross_key)))
    cross_v = low(low_back(matmul(memory, cross_value)))
    cross_bias = jnp.transpose(cross_table[cross_ids], (2, 0, 1))
    mixed_cross = attend(cross_q, cross_k, cross_v, cross_bias, None)
    after_cross = after_self + low_back(matmul(mixed_cross, cross_output))
    ffn_in = low(rms_norm(after_cross, gain_ffn))
    gate_pre = low_back(matmul(ffn_in, ffn_gate))
    up_pre = low_back(matmul(ffn_in, ffn_up))
    hidden = low(jax.nn.gelu(gate_pre, approximate=True) * up_pre)
    return after_cross + low_back(matmul(hidden, ffn_down))

def reference(inputs, memory, out_grad, gain_self, self_query, self_key, self_value, self_output, self_table, gain_cross, cross_query, cross_key, cross_value, cross_output, cross_table, gain_ffn, ffn_gate, ffn_up, ffn_down):
    params = tuple((weight.astype(jnp.float32) for weight in (gain_self, self_query, self_key, self_value, self_output, self_table, gain_cross, cross_query, cross_key, cross_value, cross_output, cross_table, gain_ffn, ffn_gate, ffn_up, ffn_down)))

    def one_sequence(totals, pieces):
        seq_in, seq_mem, seq_grad = pieces
        output, pullback = jax.vjp(forward, seq_in.astype(jnp.float32), seq_mem.astype(jnp.float32), *params)
        grad_list = pullback(seq_grad.astype(jnp.float32))
        totals = jax.tree.map(jnp.add, totals, tuple(grad_list[2:]))
        return (totals, (output.astype(jnp.bfloat16), grad_list[0], grad_list[1]))
    start_sums = tuple((jnp.zeros_like(weight) for weight in params))
    totals, stacked = lax.scan(one_sequence, start_sums, (inputs, memory, out_grad))
    return (stacked[0], stacked[1], stacked[2], totals[0], totals[1], totals[2], totals[3], totals[4], totals[5], totals[6], totals[7], totals[8], totals[9], totals[10], totals[11], totals[12], totals[13], totals[14], totals[15])
```

```python
import functools
import jax, jax.numpy as jnp
import numpy as np
from jax import lax
from jax.experimental import pallas as pl
from jax.experimental.pallas import tpu as pltpu
from jax.sharding import PartitionSpec as P

DH = 64
eps = 1e-06
QB = 256
NEG = -1e30


def mm(a, b, dims):
    return lax.dot_general(a, b, (dims, ((), ())), preferred_element_type=jnp.float32)


NN = ((1,), (0,))
NT = ((1,), (1,))
TN = ((0,), (0,))


def make_band(x_ref, far_ref, group, head, band_ref):
    tiles = []
    for d in range(3):
        row = jnp.broadcast_to(x_ref[0, 3 * head + d, :].reshape(1, 256), (128, 256))
        tiles.append(pltpu.roll(row, 0, axis=1, stride=1, stride_axis=0)[:, :128])
    left = jnp.full((128, 128), far_ref[group, 2 * head], jnp.float32)
    right = jnp.full((128, 128), far_ref[group, 2 * head + 1], jnp.float32)
    rows = [
        (left, left), (left, left), (left, left),
        (tiles[0], left), (tiles[1], tiles[0]), (tiles[2], tiles[1]), (right, tiles[2]),
        (right, right), (right, right), (right, right),
    ]
    for n, (a, b) in enumerate(rows):
        band_ref[head, n * 128:(n + 1) * 128, 0:128] = a
        band_ref[head, n * 128:(n + 1) * 128, 128:256] = b


def band_at(chunk, block):
    return pl.multiple_of((jnp.clip(chunk - block, -2, 2) + 2) * QB, QB)


def over_chunks(count, body, init):
    if isinstance(count, int):
        for c in range(count):
            init = body(c, init)
        return init
    return lax.fori_loop(0, count, body, init)


def ds(c):
    return pl.ds(pl.multiple_of(c * QB, QB), QB)


def part_sum(tile, op):
    return op(tile.reshape(QB // 8, 8, QB), axis=0)


def fwd_kernel(causal, row_ref, far_ref, x_ref, q_ref, k_ref, v_ref, o_ref, l_ref, band, keys, s_ref):
    g, r = pl.program_id(0), pl.program_id(1)
    block = r + row_ref[0]
    total_chunks = k_ref.shape[1] // QB

    @pl.when(r == 0)
    def _():
        for h in range(2):
            make_band(x_ref, far_ref, g, h, band)
        keys[...] = k_ref[...].T

    count = block + 1 if causal else total_chunks
    for h in range(2):
        q = q_ref[h * DH:(h + 1) * DH, :]

        def scores(c, top):
            s = mm(keys[ds(c), :], q, NN) + band[h, pl.ds(band_at(c, block), QB), :]
            s_ref[ds(c), :] = s
            return jnp.maximum(top, part_sum(s, jnp.max))

        top = over_chunks(count, scores, jnp.full((8, QB), NEG, jnp.float32))
        top = jnp.max(top, axis=0, keepdims=True)

        def weigh(c, tot):
            e = jnp.exp(s_ref[ds(c), :] - top)
            s_ref[ds(c), :] = e
            return tot + part_sum(e, jnp.sum)

        tot = over_chunks(count, weigh, jnp.zeros((8, QB), jnp.float32))
        tot = jnp.sum(tot, axis=0, keepdims=True)
        inv = 1.0 / tot

        def mix(c, acc):
            p = (s_ref[ds(c), :] * inv).astype(jnp.bfloat16)
            return acc + mm(v_ref[:, ds(c)], p, NN)

        acc = over_chunks(count, mix, jnp.zeros((DH, QB), jnp.float32))
        o_ref[h * DH:(h + 1) * DH, :] = acc.astype(jnp.bfloat16)
        l_ref[0, h:h + 1, :] = top + jnp.log(tot)


def bwd_kernel(causal, row_ref, far_ref, x_ref, q_ref, k_ref, v_ref, d_ref, l_ref,
               dq_ref, dk_ref, dv_ref, t_ref, band, keys, values, p_ref, g_ref, near):
    g, r = pl.program_id(0), pl.program_id(1)
    block = r + row_ref[0]
    total_chunks = k_ref.shape[1] // QB

    @pl.when(r == 0)
    def _():
        for h in range(2):
            make_band(x_ref, far_ref, g, h, band)
        keys[...] = k_ref[...].T
        values[...] = v_ref[...].T
        dk_ref[...] = jnp.zeros_like(dk_ref)
        dv_ref[...] = jnp.zeros_like(dv_ref)
        near[...] = jnp.zeros_like(near)

    count = block + 1 if causal else total_chunks
    for h in range(2):
        q = q_ref[h * DH:(h + 1) * DH, :]
        d = d_ref[h * DH:(h + 1) * DH, :]
        log_total = l_ref[0, h:h + 1, :]

        def weigh(c, dot):
            s = mm(keys[ds(c), :], q, NN) + band[h, pl.ds(band_at(c, block), QB), :]
            p = jnp.exp(s - log_total)
            dp = mm(values[ds(c), :], d, NN)
            p_ref[ds(c), :] = p
            g_ref[ds(c), :] = dp
            return dot + part_sum(p * dp, jnp.sum)

        dot = over_chunks(count, weigh, jnp.zeros((8, QB), jnp.float32))
        dot = jnp.sum(dot, axis=0, keepdims=True)

        def back(c, acc):
            p = p_ref[ds(c), :]
            low = (p * (g_ref[ds(c), :] - dot)).astype(jnp.bfloat16)
            dk_ref[:, ds(c)] += mm(q, low, NT)
            dv_ref[:, ds(c)] += mm(d, p.astype(jnp.bfloat16), NT)
            at = pl.ds(band_at(c, block), QB)
            near[h, at, :] += low.astype(jnp.float32)
            return acc + mm(k_ref[:, ds(c)], low, NN)

        acc = over_chunks(count, back, jnp.zeros((DH, QB), jnp.float32))
        dq_ref[h * DH:(h + 1) * DH, :] = acc.astype(jnp.bfloat16)

    @pl.when(r == pl.num_programs(1) - 1)
    def _():
        for h in range(2):
            def piece(n, side):
                return near[h, n * 128:(n + 1) * 128, side * 128:(side + 1) * 128]

            left = piece(3, 1) + sum(piece(n, 0) + piece(n, 1) for n in range(3))
            right = piece(6, 0) + sum(piece(n, 0) + piece(n, 1) for n in range(7, 10))
            tiles = [piece(3, 0) + piece(4, 1), piece(4, 0) + piece(5, 1), piece(5, 0) + piece(6, 1)]
            for n, tile in enumerate(tiles):
                wide = jnp.concatenate([tile, jnp.zeros_like(tile)], axis=1)
                rows = wide[0:8]
                for a in range(8, 128, 8):
                    rows = rows + pltpu.roll(wide[a:a + 8], 256 - a, axis=1)
                line = rows[0:1]
                for b in range(1, 8):
                    line = line + pltpu.roll(rows[b:b + 1], 256 - b, axis=1)
                t_ref[0, 5 * h + n:5 * h + n + 1, :] = line
            for n, far in enumerate((left, right)):
                t_ref[0, 5 * h + 3 + n:5 * h + 4 + n, 0:128] = jnp.sum(far, axis=0, keepdims=True)
                t_ref[0, 5 * h + 3 + n:5 * h + 4 + n, 128:256] = jnp.zeros((1, 128), jnp.float32)


def specs(rows, keys):
    smem = pl.BlockSpec(memory_space=pltpu.SMEM)
    return dict(
        smem=smem,
        x=pl.BlockSpec((1, 6, 256), lambda g, r: (g, 0, 0)),
        q=pl.BlockSpec((2 * DH, QB), lambda g, r: (g, r)),
        k=pl.BlockSpec((DH, keys), lambda g, r: (g, 0)),
        l=pl.BlockSpec((1, 2, QB), lambda g, r: (g, 0, r)),
        t=pl.BlockSpec((1, 10, 256), lambda g, r: (g, 0, 0)),
    )


def attend(row, far, x, q, k, v, causal):
    groups, keys, rows = k.shape[0] // DH, k.shape[1], q.shape[1]
    s = specs(rows, keys)
    elements = 2 * groups * rows * keys
    return pl.pallas_call(
        functools.partial(fwd_kernel, causal),
        out_shape=(jax.ShapeDtypeStruct(q.shape, jnp.bfloat16),
                   jax.ShapeDtypeStruct((groups, 2, rows), jnp.float32)),
        grid=(groups, rows // QB),
        in_specs=[s["smem"], s["smem"], s["x"], s["q"], s["k"], s["k"]],
        out_specs=(s["q"], s["l"]),
        scratch_shapes=[pltpu.VMEM((2, 10 * 128, 256), jnp.float32), pltpu.VMEM((keys, DH), jnp.bfloat16),
                        pltpu.VMEM((keys, QB), jnp.float32)],
        compiler_params=pltpu.CompilerParams(dimension_semantics=("arbitrary", "arbitrary"), vmem_limit_bytes=24 << 20),
        cost_estimate=pl.CostEstimate(flops=4 * DH * elements, transcendentals=elements, bytes_accessed=4 * q.size + 4 * k.size),
        name="attend",
    )(row, far, x, q, k, v)


def attend_back(row, far, x, q, k, v, d, logs, causal):
    groups, keys, rows = k.shape[0] // DH, k.shape[1], q.shape[1]
    s = specs(rows, keys)
    elements = 2 * groups * rows * keys
    return pl.pallas_call(
        functools.partial(bwd_kernel, causal),
        out_shape=(jax.ShapeDtypeStruct(q.shape, jnp.bfloat16),
                   jax.ShapeDtypeStruct(k.shape, jnp.float32),
                   jax.ShapeDtypeStruct(k.shape, jnp.float32),
                   jax.ShapeDtypeStruct((groups, 10, 256), jnp.float32)),
        grid=(groups, rows // QB),
        in_specs=[s["smem"], s["smem"], s["x"], s["q"], s["k"], s["k"], s["q"], s["l"]],
        out_specs=(s["q"], s["k"], s["k"], s["t"]),
        scratch_shapes=[pltpu.VMEM((2, 10 * 128, 256), jnp.float32), pltpu.VMEM((keys, DH), jnp.bfloat16),
                        pltpu.VMEM((keys, DH), jnp.bfloat16),
                        pltpu.VMEM((keys, QB), jnp.float32), pltpu.VMEM((keys, QB), jnp.float32),
                        pltpu.VMEM((2, 10 * 128, 256), jnp.float32)],
        compiler_params=pltpu.CompilerParams(dimension_semantics=("arbitrary", "arbitrary"), vmem_limit_bytes=32 << 20),
        cost_estimate=pl.CostEstimate(flops=10 * DH * elements, transcendentals=elements, bytes_accessed=6 * q.size + 12 * k.size),
        name="attend_back",
    )(row, far, x, q, k, v, d, logs)


MAXDIST = 128


def side_buckets(n, buckets):
    exact = buckets // 2
    scaled = np.log(np.maximum(n, 1) / exact) / np.log(MAXDIST / exact)
    far = np.minimum(exact + np.floor(scaled * (buckets - exact)).astype(np.int64), buckets - 1)
    return np.where(n < exact, n, far)


def relative_buckets(r, two_sided, buckets):
    if two_sided:
        per = buckets // 2
        return side_buckets(np.abs(r), per) + np.where(r > 0, per, 0)
    return side_buckets(np.maximum(-r, 0), buckets)


def lane_offsets():
    m = np.arange(256)
    return np.stack([128 * d - np.where(m < 128, m, m - 256) for d in (-1, 0, 1)])


def bias_vectors(table, two_sided):
    buckets, heads = table.shape
    rel = lane_offsets()
    ids = relative_buckets(rel, two_sided, buckets)
    onehot = (ids.reshape(-1)[:, None] == np.arange(buckets)[None, :])
    x = jnp.dot(jnp.asarray(onehot, jnp.bfloat16), table, preferred_element_type=jnp.float32)
    x = x.reshape(3, 256, heads)
    last = table.shape[0] - 1
    if two_sided:
        left, right = table[last // 2].astype(jnp.float32), table[last].astype(jnp.float32)
    else:
        x = jnp.where(jnp.asarray(rel > 0)[:, :, None], NEG, x)
        left, right = table[last].astype(jnp.float32), jnp.full((heads,), NEG, jnp.float32)
    x = jnp.transpose(x, (2, 0, 1)).reshape(heads // 2, 6, 256)
    far = jnp.stack([left, right], axis=1).reshape(heads // 2, 4)
    return x, far


def table_gradient(t, two_sided, buckets):
    groups = t.shape[0]
    t = t.reshape(2 * groups, 5, 256)
    rel = lane_offsets()
    ids = relative_buckets(rel, two_sided, buckets)
    onehot = np.zeros((5, 256, buckets), np.float32)
    onehot[:3] = (ids[:, :, None] == np.arange(buckets)) & (np.arange(256) != 128)[None, :, None]
    last = buckets - 1
    if two_sided:
        onehot[3, :, last // 2] = 1
        onehot[4, :, last] = 1
    else:
        onehot[:3] *= (rel <= 0)[:, :, None]
        onehot[3, :, last] = 1
    return lax.dot_general(jnp.asarray(onehot.reshape(5 * 256, buckets), jnp.bfloat16).astype(jnp.float32), t.reshape(2 * groups, 5 * 256),
                           (((0,), (1,)), ((), ())), precision=lax.Precision.HIGHEST)


def norm_rows(hidden, gain_vec):
    inv_scale = lax.rsqrt(jnp.mean(hidden * hidden, axis=-1, keepdims=True) + eps)
    return hidden * inv_scale * gain_vec


def inner_rows(left_mat, right_mat):
    return lax.dot_general(
        left_mat, right_mat, (((0,), (0,)), ((), ())), preferred_element_type=jnp.float32
    )


def outer_cols(left_mat, right_mat):
    return lax.dot_general(
        left_mat, right_mat, (((1,), (1,)), ((), ())), preferred_element_type=jnp.float32
    )


def gate_times_up(gate_value, up_value):
    return jax.nn.gelu(gate_value, approximate=True) * up_value


def on_device(
    inputs,
    memory,
    out_grad,
    gain_self,
    self_query,
    self_key,
    self_value,
    self_output,
    self_table,
    gain_cross,
    cross_query,
    cross_key,
    cross_value,
    cross_output,
    cross_table,
    gain_ffn,
    ffn_gate,
    ffn_up,
    ffn_down,
):
    seq_len = inputs.shape[1]
    model_width = inputs.shape[2]
    rows_here = inputs.shape[0] * seq_len
    flat_in = inputs.reshape(rows_here, model_width).astype(jnp.float32)
    flat_mem = memory.reshape(memory.shape[0] * memory.shape[1], model_width)
    gain_one = gain_self.astype(jnp.float32)
    gain_two = gain_cross.astype(jnp.float32)
    gain_three = gain_ffn.astype(jnp.float32)
    attn_in = norm_rows(flat_in, gain_one).astype(jnp.bfloat16)
    row = jnp.zeros((1,), jnp.int32)
    self_x, self_far = bias_vectors(self_table, False)
    cross_x, cross_far = bias_vectors(cross_table, True)
    queries = mm(self_query, attn_in, ((0,), (1,))).astype(jnp.bfloat16)
    self_keys = mm(self_key, attn_in, ((0,), (1,))).astype(jnp.bfloat16)
    self_values = mm(self_value, attn_in, ((0,), (1,))).astype(jnp.bfloat16)
    mixed_self, total_self = attend(
        row, self_far, self_x, queries, self_keys, self_values, True
    )
    after_self = flat_in + lax.psum(
        mm(mixed_self, self_output, TN), "kv"
    )
    cross_in = norm_rows(after_self, gain_two).astype(jnp.bfloat16)
    cross_q = mm(cross_query, cross_in, ((0,), (1,))).astype(jnp.bfloat16)
    cross_k = mm(cross_key, flat_mem, ((0,), (1,))).astype(jnp.bfloat16)
    cross_v = mm(cross_value, flat_mem, ((0,), (1,))).astype(jnp.bfloat16)
    mixed_cross, total_cross = attend(
        row, cross_far, cross_x, cross_q, cross_k, cross_v, False
    )
    after_cross = after_self + lax.psum(
        mm(mixed_cross, cross_output, TN), "kv"
    )
    ffn_in = norm_rows(after_cross, gain_three).astype(jnp.bfloat16)
    gate_pre = jnp.dot(ffn_in, ffn_gate, preferred_element_type=jnp.float32)
    up_pre = jnp.dot(ffn_in, ffn_up, preferred_element_type=jnp.float32)
    hidden = gate_times_up(gate_pre, up_pre).astype(jnp.bfloat16)
    result = after_cross + lax.psum(
        jnp.dot(hidden, ffn_down, preferred_element_type=jnp.float32), "kv"
    )
    layer_out = result.astype(jnp.bfloat16).reshape(inputs.shape)
    grad_out = out_grad.reshape(rows_here, model_width).astype(jnp.float32)
    branch_grad = grad_out.astype(jnp.bfloat16)
    grad_down = inner_rows(hidden, branch_grad)
    hidden_grad = outer_cols(branch_grad, ffn_down)
    gate_grad, up_grad = jax.vjp(gate_times_up, gate_pre, up_pre)[1](hidden_grad)
    gate_low = gate_grad.astype(jnp.bfloat16)
    up_low = up_grad.astype(jnp.bfloat16)
    grad_gate = inner_rows(ffn_in, gate_low)
    grad_up = inner_rows(ffn_in, up_low)
    ffn_in_grad = lax.psum(outer_cols(gate_low, ffn_gate) + outer_cols(up_low, ffn_up), "kv")
    norm_grad, grad_gain_ffn = jax.vjp(norm_rows, after_cross, gain_three)[1](ffn_in_grad)
    cross_out_grad = grad_out + norm_grad
    ffn_parts = lax.psum((grad_gain_ffn, grad_gate, grad_up, grad_down), "batch")
    branch_grad = cross_out_grad.astype(jnp.bfloat16)
    grad_cross_out = mm(mixed_cross, branch_grad, NN)
    mixed_grad = mm(cross_output, branch_grad, NT).astype(jnp.bfloat16)
    cq_grad, ck_grad, cv_grad, cross_lines = attend_back(
        row, cross_far, cross_x, cross_q, cross_k, cross_v, mixed_grad, total_cross, False
    )
    ck_grad, cv_grad = ck_grad.astype(jnp.bfloat16), cv_grad.astype(jnp.bfloat16)
    grad_cross_tab = table_gradient(cross_lines, True, cross_table.shape[0])
    grad_cq = mm(cross_in, cq_grad, ((0,), (1,)))
    grad_ck = mm(flat_mem, ck_grad, ((0,), (1,)))
    grad_cv = mm(flat_mem, cv_grad, ((0,), (1,)))
    cross_in_grad = lax.psum(mm(cq_grad, cross_query, ((0,), (1,))), "kv")
    memory_term = mm(ck_grad, cross_key, ((0,), (1,))) + mm(cv_grad, cross_value, ((0,), (1,)))
    memory_grad = lax.psum_scatter(
        memory_term.reshape(memory.shape), "kv", scatter_dimension=2, tiled=True
    )
    norm_grad, grad_gain_cross = jax.vjp(norm_rows, after_self, gain_two)[1](cross_in_grad)
    self_out_grad = cross_out_grad + norm_grad
    cross_parts = lax.psum(
        (grad_gain_cross, grad_cq, grad_ck, grad_cv, grad_cross_out, grad_cross_tab), "batch"
    )
    branch_grad = self_out_grad.astype(jnp.bfloat16)
    grad_self_out = mm(mixed_self, branch_grad, NN)
    mixed_grad = mm(self_output, branch_grad, NT).astype(jnp.bfloat16)
    sq_grad, sk_grad, sv_grad, self_lines = attend_back(
        row, self_far, self_x, queries, self_keys, self_values, mixed_grad, total_self, True
    )
    sk_grad, sv_grad = sk_grad.astype(jnp.bfloat16), sv_grad.astype(jnp.bfloat16)
    grad_self_tab = table_gradient(self_lines, False, self_table.shape[0])
    grad_sq = mm(attn_in, sq_grad, ((0,), (1,)))
    grad_sk = mm(attn_in, sk_grad, ((0,), (1,)))
    grad_sv = mm(attn_in, sv_grad, ((0,), (1,)))
    attn_term = (
        mm(sq_grad, self_query, ((0,), (1,)))
        + mm(sk_grad, self_key, ((0,), (1,)))
        + mm(sv_grad, self_value, ((0,), (1,)))
    )
    attn_in_grad = lax.psum(attn_term, "kv")
    norm_grad, grad_gain_self = jax.vjp(norm_rows, flat_in, gain_one)[1](attn_in_grad)
    input_grad = (self_out_grad + norm_grad).reshape(inputs.shape)
    self_parts = lax.psum(
        (grad_gain_self, grad_sq, grad_sk, grad_sv, grad_self_out, grad_self_tab), "batch"
    )
    summed = tuple(self_parts) + tuple(cross_parts) + tuple(ffn_parts)
    return (
        layer_out,
        input_grad,
        memory_grad,
        summed[0],
        summed[1],
        summed[2],
        summed[3],
        summed[4],
        summed[5],
        summed[6],
        summed[7],
        summed[8],
        summed[9],
        summed[10],
        summed[11],
        summed[12],
        summed[13],
        summed[14],
        summed[15],
    )


def solution(mesh):
    return jax.shard_map(
        on_device,
        mesh=mesh,
        in_specs=(
            P("batch", None, None),
            P("batch", None, None),
            P("batch", None, None),
            P(),
            P(None, "kv"),
            P(None, "kv"),
            P(None, "kv"),
            P("kv", None),
            P(None, "kv"),
            P(),
            P(None, "kv"),
            P(None, "kv"),
            P(None, "kv"),
            P("kv", None),
            P(None, "kv"),
            P(),
            P(None, "kv"),
            P(None, "kv"),
            P("kv", None),
        ),
        out_specs=(
            P("batch", None, None),
            P("batch", None, None),
            P("batch", None, "kv"),
            P(),
            P(None, "kv"),
            P(None, "kv"),
            P(None, "kv"),
            P("kv", None),
            P(None, "kv"),
            P(),
            P(None, "kv"),
            P(None, "kv"),
            P(None, "kv"),
            P("kv", None),
            P(None, "kv"),
            P(),
            P(None, "kv"),
            P(None, "kv"),
            P("kv", None),
        ),
        check_vma=False,
    )
```

```python
import functools
import jax, jax.numpy as jnp
import numpy as np
from jax import lax
from jax.experimental import pallas as pl
from jax.experimental.pallas import tpu as pltpu
from jax.sharding import PartitionSpec as P

DH = 64
eps = 1e-06
QB = 256
NEG = -1e30


def cost(scores, weight):
    return pl.CostEstimate(flops=0, transcendentals=0, bytes_accessed=scores * weight)


def mm(a, b, dims):
    return lax.dot_general(a, b, (dims, ((), ())), preferred_element_type=jnp.float32)


NN = ((1,), (0,))
NT = ((1,), (1,))
TN = ((0,), (0,))


def make_band(x_ref, head, band_ref):
    tiles = []
    for d in range(3):
        row = jnp.broadcast_to(x_ref[0, 3 * head + d, :].reshape(1, 256), (128, 256))
        tiles.append(pltpu.roll(row, 0, axis=1, stride=1, stride_axis=0)[:, :128])
    left = jnp.broadcast_to(x_ref[0, 6 + head, 0:128].reshape(1, 128), (128, 128))
    right = jnp.broadcast_to(x_ref[0, 6 + head, 128:256].reshape(1, 128), (128, 128))
    rows = [
        (left, left), (left, left), (left, left),
        (tiles[0], left), (tiles[1], tiles[0]), (tiles[2], tiles[1]), (right, tiles[2]),
        (right, right), (right, right), (right, right),
    ]
    for n, (a, b) in enumerate(rows):
        band_ref[head, n * 128:(n + 1) * 128, 0:128] = a
        band_ref[head, n * 128:(n + 1) * 128, 128:256] = b


def band_at(chunk, block):
    return pl.multiple_of((jnp.clip(chunk - block, -2, 2) + 2) * QB, QB)


def over_chunks(count, body, init):
    if isinstance(count, int):
        for c in range(count):
            init = body(c, init)
        return init
    return lax.fori_loop(0, count, body, init)


def ds(c):
    return pl.ds(pl.multiple_of(c * QB, QB), QB)


def part_sum(tile, op):
    return op(tile.reshape(QB // 8, 8, QB), axis=0)


def fwd_kernel(causal, row_ref, x_ref, q_ref, k_ref, v_ref, o_ref, l_ref, band, keys, s_ref):
    r = pl.program_id(1)
    block = r + row_ref[0]
    total_chunks = k_ref.shape[1] // QB

    @pl.when(r == 0)
    def _():
        for h in range(2):
            make_band(x_ref, h, band)
        keys[...] = k_ref[...].T

    count = block + 1 if causal else total_chunks
    for h in range(2):
        q = q_ref[h * DH:(h + 1) * DH, :]

        def scores(c, top):
            s = mm(keys[ds(c), :], q, NN) + band[h, pl.ds(band_at(c, block), QB), :]
            s_ref[ds(c), :] = s
            return jnp.maximum(top, part_sum(s, jnp.max))

        top = over_chunks(count, scores, jnp.full((8, QB), NEG, jnp.float32))
        top = jnp.max(top, axis=0, keepdims=True)

        def weigh(c, tot):
            e = jnp.exp(s_ref[ds(c), :] - top)
            s_ref[ds(c), :] = e
            return tot + part_sum(e, jnp.sum)

        tot = over_chunks(count, weigh, jnp.zeros((8, QB), jnp.float32))
        tot = jnp.sum(tot, axis=0, keepdims=True)
        inv = 1.0 / tot

        def mix(c, acc):
            p = (s_ref[ds(c), :] * inv).astype(jnp.bfloat16)
            return acc + mm(v_ref[:, ds(c)], p, NN)

        acc = over_chunks(count, mix, jnp.zeros((DH, QB), jnp.float32))
        o_ref[h * DH:(h + 1) * DH, :] = acc.astype(jnp.bfloat16)
        l_ref[0, h:h + 1, :] = top + jnp.log(tot)


def bwd_kernel(causal, row_ref, x_ref, q_ref, k_ref, v_ref, d_ref, l_ref,
               dq_ref, dk_ref, dv_ref, t_ref, band, keys, values, p_ref, g_ref, near):
    r = pl.program_id(1)
    block = r + row_ref[0]
    total_chunks = k_ref.shape[1] // QB

    @pl.when(r == 0)
    def _():
        for h in range(2):
            make_band(x_ref, h, band)
        keys[...] = k_ref[...].T
        values[...] = v_ref[...].T
        dk_ref[...] = jnp.zeros_like(dk_ref)
        dv_ref[...] = jnp.zeros_like(dv_ref)
        near[...] = jnp.zeros_like(near)

    count = block + 1 if causal else total_chunks
    for h in range(2):
        q = q_ref[h * DH:(h + 1) * DH, :]
        d = d_ref[h * DH:(h + 1) * DH, :]
        log_total = l_ref[0, h:h + 1, :]

        def weigh(c, dot):
            s = mm(keys[ds(c), :], q, NN) + band[h, pl.ds(band_at(c, block), QB), :]
            p = jnp.exp(s - log_total)
            dp = mm(values[ds(c), :], d, NN)
            p_ref[ds(c), :] = p
            g_ref[ds(c), :] = dp
            return dot + part_sum(p * dp, jnp.sum)

        dot = over_chunks(count, weigh, jnp.zeros((8, QB), jnp.float32))
        dot = jnp.sum(dot, axis=0, keepdims=True)

        def back(c, acc):
            p = p_ref[ds(c), :]
            low = (p * (g_ref[ds(c), :] - dot)).astype(jnp.bfloat16)
            dk_ref[:, ds(c)] += mm(q, low, NT)
            dv_ref[:, ds(c)] += mm(d, p.astype(jnp.bfloat16), NT)
            at = pl.ds(band_at(c, block), QB)
            near[h, at, :] += low.astype(jnp.float32)
            return acc + mm(k_ref[:, ds(c)], low, NN)

        acc = over_chunks(count, back, jnp.zeros((DH, QB), jnp.float32))
        dq_ref[h * DH:(h + 1) * DH, :] = acc.astype(jnp.bfloat16)

    @pl.when(r == pl.num_programs(1) - 1)
    def _():
        for h in range(2):
            def piece(n, side):
                return near[h, n * 128:(n + 1) * 128, side * 128:(side + 1) * 128]

            left = piece(3, 1) + sum(piece(n, 0) + piece(n, 1) for n in range(3))
            right = piece(6, 0) + sum(piece(n, 0) + piece(n, 1) for n in range(7, 10))
            tiles = [piece(3, 0) + piece(4, 1), piece(4, 0) + piece(5, 1), piece(5, 0) + piece(6, 1)]
            for n, tile in enumerate(tiles):
                wide = jnp.concatenate([tile, jnp.zeros_like(tile)], axis=1)
                rows = wide[0:8]
                for a in range(8, 128, 8):
                    rows = rows + pltpu.roll(wide[a:a + 8], 256 - a, axis=1)
                line = rows[0:1]
                for b in range(1, 8):
                    line = line + pltpu.roll(rows[b:b + 1], 256 - b, axis=1)
                t_ref[0, 5 * h + n:5 * h + n + 1, :] = line
            for n, far in enumerate((left, right)):
                t_ref[0, 5 * h + 3 + n:5 * h + 4 + n, 0:128] = jnp.sum(far, axis=0, keepdims=True)
                t_ref[0, 5 * h + 3 + n:5 * h + 4 + n, 128:256] = jnp.zeros((1, 128), jnp.float32)


def specs(rows, keys):
    smem = pl.BlockSpec(memory_space=pltpu.SMEM)
    return dict(
        smem=smem,
        x=pl.BlockSpec((1, 8, 256), lambda g, r: (g, 0, 0)),
        q=pl.BlockSpec((2 * DH, QB), lambda g, r: (g, r)),
        k=pl.BlockSpec((DH, keys), lambda g, r: (4 * (g // 2) + g % 2, 0)),
        v=pl.BlockSpec((DH, keys), lambda g, r: (4 * (g // 2) + g % 2 + 2, 0)),
        dk=pl.BlockSpec((DH, keys), lambda g, r: (g, 0)),
        l=pl.BlockSpec((1, 2, QB), lambda g, r: (g, 0, r)),
        t=pl.BlockSpec((1, 10, 256), lambda g, r: (g, 0, 0)),
    )


def attend(row, x, q, kv, causal):
    groups, keys, rows = kv.shape[0] // (2 * DH), kv.shape[1], q.shape[1]
    s = specs(rows, keys)
    return pl.pallas_call(
        functools.partial(fwd_kernel, causal),
        out_shape=(jax.ShapeDtypeStruct(q.shape, jnp.bfloat16),
                   jax.ShapeDtypeStruct((groups, 2, rows), jnp.float32)),
        grid=(groups, rows // QB),
        in_specs=[s["smem"], s["x"], s["q"], s["k"], s["v"]],
        out_specs=(s["q"], s["l"]),
        scratch_shapes=[pltpu.VMEM((2, 10 * 128, 256), jnp.float32), pltpu.VMEM((keys, DH), jnp.bfloat16),
                        pltpu.VMEM((keys, QB), jnp.float32)],
        compiler_params=pltpu.CompilerParams(dimension_semantics=("arbitrary", "arbitrary"), vmem_limit_bytes=24 << 20),
        cost_estimate=cost(2 * groups * rows * keys, 11),
        name="attend",
    )(row, x, q, kv, kv)


def attend_back(row, x, q, kv, d, logs, causal):
    groups, keys, rows = kv.shape[0] // (2 * DH), kv.shape[1], q.shape[1]
    s = specs(rows, keys)
    return pl.pallas_call(
        functools.partial(bwd_kernel, causal),
        out_shape=(jax.ShapeDtypeStruct(q.shape, jnp.bfloat16),
                   jax.ShapeDtypeStruct((groups * DH, keys), jnp.float32),
                   jax.ShapeDtypeStruct((groups * DH, keys), jnp.float32),
                   jax.ShapeDtypeStruct((groups, 10, 256), jnp.float32)),
        grid=(groups, rows // QB),
        in_specs=[s["smem"], s["x"], s["q"], s["k"], s["v"], s["q"], s["l"]],
        out_specs=(s["q"], s["dk"], s["dk"], s["t"]),
        scratch_shapes=[pltpu.VMEM((2, 10 * 128, 256), jnp.float32), pltpu.VMEM((keys, DH), jnp.bfloat16),
                        pltpu.VMEM((keys, DH), jnp.bfloat16),
                        pltpu.VMEM((keys, QB), jnp.float32), pltpu.VMEM((keys, QB), jnp.float32),
                        pltpu.VMEM((2, 10 * 128, 256), jnp.float32)],
        compiler_params=pltpu.CompilerParams(dimension_semantics=("arbitrary", "arbitrary"), vmem_limit_bytes=32 << 20),
        cost_estimate=cost(2 * groups * rows * keys, 18),
        name="attend_back",
    )(row, x, q, kv, kv, d, logs)


MAXDIST = 128


def side_buckets(n, buckets):
    exact = buckets // 2
    scaled = np.log(np.maximum(n, 1) / exact) / np.log(MAXDIST / exact)
    far = np.minimum(exact + np.floor(scaled * (buckets - exact)).astype(np.int64), buckets - 1)
    return np.where(n < exact, n, far)


def relative_buckets(r, two_sided, buckets):
    if two_sided:
        per = buckets // 2
        return side_buckets(np.abs(r), per) + np.where(r > 0, per, 0)
    return side_buckets(np.maximum(-r, 0), buckets)


def lane_offsets():
    m = np.arange(256)
    return np.stack([128 * d - np.where(m < 128, m, m - 256) for d in (-1, 0, 1)])


def bias_vectors(table, two_sided):
    buckets, heads = table.shape
    rel = lane_offsets()
    ids = relative_buckets(rel, two_sided, buckets)
    onehot = (ids.reshape(-1)[:, None] == np.arange(buckets)[None, :])
    x = jnp.dot(jnp.asarray(onehot, jnp.bfloat16), table, preferred_element_type=jnp.float32)
    x = x.reshape(3, 256, heads)
    last = table.shape[0] - 1
    if two_sided:
        left, right = table[last // 2].astype(jnp.float32), table[last].astype(jnp.float32)
    else:
        x = jnp.where(jnp.asarray(rel > 0)[:, :, None], NEG, x)
        left, right = table[last].astype(jnp.float32), jnp.full((heads,), NEG, jnp.float32)
    x = jnp.transpose(x, (2, 0, 1)).reshape(heads // 2, 6, 256)
    far = jnp.stack([left, right], axis=1).reshape(heads // 2, 2, 2, 1)
    return jnp.concatenate([x, jnp.broadcast_to(far, far.shape[:3] + (128,)).reshape(heads // 2, 2, 256)], axis=1)


def table_gradient(t, two_sided, buckets):
    groups = t.shape[0]
    t = t.reshape(2 * groups, 5, 256)
    rel = lane_offsets()
    ids = relative_buckets(rel, two_sided, buckets)
    onehot = np.zeros((5, 256, buckets), np.float32)
    onehot[:3] = (ids[:, :, None] == np.arange(buckets)) & (np.arange(256) != 128)[None, :, None]
    last = buckets - 1
    if two_sided:
        onehot[3, :, last // 2] = 1
        onehot[4, :, last] = 1
    else:
        onehot[:3] *= (rel <= 0)[:, :, None]
        onehot[3, :, last] = 1
    return lax.dot_general(jnp.asarray(onehot.reshape(5 * 256, buckets), jnp.bfloat16).astype(jnp.float32), t.reshape(2 * groups, 5 * 256),
                           (((0,), (1,)), ((), ())), precision=lax.Precision.HIGHEST)


def norm_rows(hidden, gain_vec):
    inv_scale = lax.rsqrt(jnp.mean(hidden * hidden, axis=-1, keepdims=True) + eps)
    return hidden * inv_scale * gain_vec


def gate_times_up(gate_value, up_value):
    return jax.nn.gelu(gate_value, approximate=True) * up_value


T0 = ((0,), (1,))


def block_of(x, index, size, axis=0):
    return lax.dynamic_slice_in_dim(x, index * size, size, axis)


class Gather:
    def __init__(self, x, n):
        self.n, self.x, self.d = n, x, 0
        self.right = self.left = x
        self.from_left, self.from_right = [], []

    def hop(self, tie, *others):
        n, self.d = self.n, self.d + 1
        d = self.d
        self.right = lax.ppermute(tie(self.right, *others), "kv", [(i, i + 1) for i in range(d - 1, n - 1)])
        self.left = lax.ppermute(tie(self.left, *others), "kv", [(i + 1, i) for i in range(n - d)])
        self.from_left.append(self.right)
        self.from_right.append(self.left)
        return [self.right, self.left]

    def blocks(self):
        n = self.n
        return [self.x] + [self.from_right[d - 1] + self.from_left[n - d - 1] for d in range(1, n)]


class Scatter:
    def __init__(self, parts, n):
        self.n, self.parts, self.d = n, parts, n
        self.got = [0.0, 0.0]

    def hop(self, tie, *others):
        n, self.d = self.n, self.d - 1
        d = self.d
        right, left = self.parts[d] + self.got[0], self.parts[n - d] + self.got[1]
        self.got = [
            lax.ppermute(tie(right, *others), "kv", [(i, i + 1) for i in range(n - d)]),
            lax.ppermute(tie(left, *others), "kv", [(i + 1, i) for i in range(d - 1, n - 1)]),
        ]
        return self.got

    def total(self):
        return self.parts[0] + self.got[0] + self.got[1]


def in_order(blocks, z, n):
    stacked = jnp.stack(blocks)
    return jnp.concatenate(
        [lax.dynamic_index_in_dim(stacked, (j - z + n) % n, 0, keepdims=False) for j in range(n)]
    )


def exchange(blocks, n):
    got = [blocks[0]]
    for d in range(1, n):
        got.append(lax.ppermute(blocks[n - d], "kv", [((i + d) % n, i) for i in range(n)]))
    return got


def whole_kernel(thin, deep, shares_ref, in_ref, so_ref, co_ref, *refs):
    so_out, co_out, cq_out, kv_out = refs[-4:]
    d = pl.program_id(0)
    half = shares_ref.shape[3]
    qcols = cq_out.shape[2]

    @pl.when(d == 0)
    def _():
        so_out[...] = so_ref[...]
        co_out[...] = co_ref[...]
        cq_out[0] = in_ref[:, :qcols]
        kv_out[0] = in_ref[:, qcols:]

    @pl.when(d > 0)
    def _():
        for i in range(shares_ref.shape[0]):
            here = shares_ref[i, 0, 0:deep, :].astype(jnp.bfloat16)
            cq_out[0, i * deep:(i + 1) * deep, :] = here[:, :qcols]
            kv_out[0, i * deep:(i + 1) * deep, :] = here[:, qcols:]
            for n, ref in enumerate((so_out, co_out)):
                for side in range(2):
                    at = deep + (2 * n + side) * thin
                    ref[i * thin:(i + 1) * thin, side * half:(side + 1) * half] = (
                        shares_ref[i, 0, at:at + thin, :].astype(jnp.bfloat16)
                    )


def whole_weights(shares, own_in, own_so, own_co, earlier):
    nb, others = shares.shape[:2]
    width, cols = own_in.shape
    tall = own_so.shape[0]
    step = 4
    turns = nb // step
    own = lambda d, i: (jnp.where(d == 0, i, turns - 1), 0)
    flat = pl.BlockSpec((tall // turns, width), lambda d, i: (d * turns + i, 0))
    deep = pl.BlockSpec((1, width // turns, cols // 2), lambda d, i: (d, i, 0))
    return pl.pallas_call(
        functools.partial(whole_kernel, tall // nb, width // nb),
        out_shape=(jax.ShapeDtypeStruct(((others + 1) * tall, width), jnp.bfloat16),) * 2
        + (jax.ShapeDtypeStruct((others + 1, width, cols // 2), jnp.bfloat16),) * 2,
        grid=(others + 1, turns),
        in_specs=[
            pl.BlockSpec((step, 1) + shares.shape[2:], lambda d, i: (jnp.where(d == 0, 0, i), jnp.maximum(d - 1, 0), 0, 0)),
            pl.BlockSpec((width // turns, cols), own),
            pl.BlockSpec((tall // turns, width), own),
            pl.BlockSpec((tall // turns, width), own),
        ] + [pl.BlockSpec((16, 128), lambda d, i: (0, 0))] * len(earlier),
        out_specs=(flat, flat, deep, deep),
        compiler_params=pltpu.CompilerParams(dimension_semantics=("arbitrary", "arbitrary"), vmem_limit_bytes=32 << 20),
        cost_estimate=cost(shares.size, 7),
        name="whole_weights",
    )(shares, own_in, own_so, own_co, *earlier)


def on_device(
    inputs,
    memory,
    out_grad,
    gain_self,
    self_query,
    self_key,
    self_value,
    self_output,
    self_table,
    gain_cross,
    cross_query,
    cross_key,
    cross_value,
    cross_output,
    cross_table,
    gain_ffn,
    ffn_gate,
    ffn_up,
    ffn_down,
):
    seq_len = inputs.shape[1]
    width = inputs.shape[2]
    n, nb = lax.axis_size("kv"), lax.axis_size("batch")
    z, b = lax.axis_index("kv"), lax.axis_index("batch")
    rows = seq_len // n
    low = jnp.bfloat16
    one = jnp.where(gain_self[0] < 100, 1.0, 2.0).astype(jnp.float32)

    def settle(x):
        return x * one

    def tie(x, *others):
        for other in others:
            x = x + other[(0,) * other.ndim].astype(jnp.float32) * (one - 1.0)
        return x

    def share(w):
        return block_of(w, b, w.shape[0] // nb).astype(jnp.float32)

    def halves(x):
        return jnp.concatenate([x[:, :width // 2], x[:, width // 2:]])

    qcols, kcols, ocols = cross_query.shape[1], cross_key.shape[1], cross_output.shape[0]
    far_pairs = [(i, i ^ 2) for i in range(n)]
    near_pairs = [(i, i ^ 1) for i in range(n)]
    cross_kv = jnp.concatenate([cross_key, cross_value], axis=1)
    unit = jnp.concatenate(
        [
            jnp.concatenate([share(cross_query), share(cross_kv)], axis=1),
            halves(share(self_output)),
            halves(share(cross_output)),
        ]
    )
    units = exchange([unit] * n, n)[1:]

    gain_one = gain_self.astype(jnp.float32)
    gain_two = gain_cross.astype(jnp.float32)
    gain_three = gain_ffn.astype(jnp.float32)
    self_x, own_cross_x = bias_vectors(self_table, False), bias_vectors(cross_table, True)

    flat_in = inputs.reshape(seq_len, width).astype(jnp.float32)
    flat_mem = memory.reshape(memory.shape[1], width)
    attn_in = norm_rows(flat_in, gain_one).astype(low)
    zero = jnp.zeros((1,), jnp.int32)
    self_kv = jnp.concatenate([self_key, self_value], axis=1)
    sq = mm(self_query, attn_in, T0).astype(low)
    skv = mm(self_kv, attn_in, T0).astype(low)
    mixed, self_log = attend(zero, self_x, sq, skv, True)
    buckets, heads = self_table.shape
    deep, thin = width // nb, ocols // nb
    shares = lax.all_gather(tie(jnp.stack(units), mixed), "batch")
    mixed = tie(mixed.astype(jnp.float32), *units)
    rider = own_cross_x.reshape(-1, rows)
    got = exchange([jnp.concatenate([block_of(mixed, (z + d) % n, rows, 1), rider]) for d in range(n)], n)
    others = got[1:]
    mixed_self = settle(jnp.concatenate([x[:ocols] for x in got])).astype(low)
    cross_x = jnp.concatenate([x[ocols:] for x in got]).reshape(-1, 8, rows)
    own_in = jnp.concatenate([cross_query, cross_kv], axis=1)
    whole_so, whole_co, whole_cq, whole_kv = whole_weights(
        shares, own_in, self_output, cross_output, [mixed_self, cross_x.reshape(-1, rows)]
    )

    sent = jnp.stack([share(ffn_gate.T), share(ffn_up.T), share(ffn_down)])
    fetched = lax.ppermute(tie(sent, *others), "kv", far_pairs)
    sent = lax.all_gather(tie(fetched, whole_so), "batch", axis=1, tiled=True)

    in_rows = block_of(flat_in, z, rows)
    after_self = in_rows + mm(mixed_self, whole_so, TN)

    def into(w, x):
        y = lax.dot_general(w, x, (((1,), (1,)), ((), ())), preferred_element_type=jnp.float32)
        return y.astype(low).reshape(-1, x.shape[0])

    ckv = into(whole_kv, flat_mem)
    cross_in = norm_rows(after_self, gain_two).astype(low)
    cq = into(whole_cq, cross_in)
    place = z.reshape(1).astype(jnp.int32) * (rows // QB)
    mixed_cross, cross_log = attend(place, cross_x, cq, ckv, False)
    after_cross = after_self + mm(mixed_cross, whole_co, TN)

    own_self = jnp.concatenate([self_query, self_kv], axis=1)
    unit = tie(jnp.concatenate([share(self_query), share(self_kv)], axis=1), fetched)
    rest_self = lax.all_gather(tie(jnp.stack(exchange([unit] * n, n)[1:]), after_cross), "batch", axis=1, tiled=True)
    rest_self = settle(rest_self).astype(low)

    ffn_in = norm_rows(after_cross, gain_three).astype(low)
    other = settle(lax.ppermute(ffn_in.astype(jnp.float32), "kv", near_pairs)).astype(low)
    flat_grad = out_grad.reshape(seq_len, width)
    own_grad = block_of(flat_grad, z, rows)
    far_ffn = settle(sent).astype(low)
    weights = ((ffn_gate, ffn_up, ffn_down, False), (far_ffn[0], far_ffn[1], far_ffn[2], True))
    parts, grads, inputs_of = [], [], ((ffn_in, own_grad), (other, block_of(flat_grad, z ^ 1, rows)))
    for x, dy in inputs_of:
        in_part = out_part = 0.0
        for w_gate, w_up, w_down, turned in weights:
            there, back = (NT, NN) if turned else (NN, NT)
            gate_pre, up_pre = mm(x, w_gate, there), mm(x, w_up, there)
            hidden = gate_times_up(gate_pre, up_pre).astype(low)
            out_part = out_part + mm(hidden, w_down, NN)
            gate_grad, up_grad = jax.vjp(gate_times_up, gate_pre, up_pre)[1](mm(dy, w_down, NT))
            gate_grad, up_grad = gate_grad.astype(low), up_grad.astype(low)
            in_part = in_part + mm(gate_grad, w_gate, back) + mm(up_grad, w_up, back)
            grads.append((gate_grad, up_grad, hidden))
        parts.append((in_part, out_part))
    ffn_in_grad = parts[0][0] + lax.ppermute(parts[1][0], "kv", near_pairs)
    both_in, both_grad = (jnp.concatenate(x) for x in zip(*inputs_of))
    ffn_sums = jnp.stack(
        [
            mm(jnp.concatenate([grads[side][kind], grads[2 + side][kind]]), both_grad if kind == 2 else both_in, TN)
            for side in range(2) for kind in range(3)
        ]
    )
    ffn_sums = lax.psum_scatter(ffn_sums, "batch", scatter_dimension=1, tiled=True)
    ffn_out = parts[0][1] + lax.ppermute(tie(parts[1][1], ffn_in_grad), "kv", near_pairs)

    norm_grad, grad_gain_ffn = jax.vjp(norm_rows, after_cross, gain_three)[1](ffn_in_grad)
    cross_out_grad = own_grad.astype(jnp.float32) + norm_grad
    branch_cross = cross_out_grad.astype(low)
    mixed_grad = mm(whole_co, branch_cross, NT).astype(low)
    cq_grad, ck_grad, cv_grad, cross_lines = attend_back(
        place, cross_x, cq, ckv, mixed_grad, cross_log, False
    )
    result = (tie(after_cross, cq_grad) + ffn_out).astype(low).astype(jnp.float32)
    line = Gather(result, n)
    first = line.hop(tie)
    cross_in_grad = lax.dot_general(
        cq_grad.reshape(n, qcols, rows), whole_cq, (((0, 1), (0, 2)), ((), ())), preferred_element_type=jnp.float32
    )
    norm_grad, grad_gain_cross = jax.vjp(norm_rows, after_self, gain_two)[1](cross_in_grad)
    self_out_grad = cross_out_grad + norm_grad
    branch_self = self_out_grad.astype(low)
    mixed_grad = tie(mm(whole_so, branch_self, NT).astype(low).astype(jnp.float32), result)
    got = exchange([mixed_grad[d * ocols:(d + 1) * ocols] for d in range(n)], n)
    arrived = got[1:]
    stacked = jnp.stack(got)
    mixed_grad = tie(
        jnp.concatenate(
            [lax.dynamic_index_in_dim(stacked, (j - z + n) % n, 0, keepdims=False) for j in range(n)], axis=1
        ),
        *first,
    )
    mixed_grad = settle(mixed_grad).astype(low)
    ckv_grad = jnp.concatenate(
        [ck_grad.reshape(n, kcols, -1), cv_grad.reshape(n, kcols, -1)], axis=1
    ).astype(low)
    memory_part = [
        lax.dot_general(ckv_grad, block_of(whole_kv, (z + d) % n, width // n, 1),
                        (((0, 1), (0, 2)), ((), ())), preferred_element_type=jnp.float32)
        for d in range(n)
    ]

    sq_grad, sk_grad, sv_grad, self_lines = attend_back(zero, self_x, sq, skv, mixed_grad, self_log, True)
    skv_grad = jnp.concatenate([sk_grad, sv_grad]).astype(low)
    memory_line = Scatter(memory_part, n)
    second, memory_one = line.hop(tie), memory_line.hop(tie)
    turned = jnp.concatenate([sq_grad, skv_grad]).astype(jnp.float32)
    got = exchange([tie(block_of(turned, (z + d) % n, rows, 1), *second, *memory_one) for d in range(n)], n)
    rest = settle(jnp.stack(got[1:])).astype(low)
    attn_in_grad = mm(got[0].astype(low), own_self, T0) + lax.dot_general(
        rest, rest_self, (((0, 1), (0, 2)), ((), ())), preferred_element_type=jnp.float32
    )
    early = got[1:]
    third, memory_two = line.hop(tie), memory_line.hop(tie)
    attn_term = mm(sq_grad, self_query, T0) + mm(skv_grad, self_kv, T0)
    norm_grad, _ = jax.vjp(norm_rows, in_rows, gain_one)[1](attn_in_grad)
    last = tie(self_out_grad + norm_grad, *third, *memory_two)
    _, grad_gain_self = jax.vjp(norm_rows, flat_in, gain_one)[1](attn_term)

    ends_line = Gather(last, n)
    one_hop = ends_line.hop(tie)
    memory_three = memory_line.hop(tie)
    two_hops = ends_line.hop(tie)
    ends_line.hop(tie)
    layer_out = settle(in_order(line.blocks(), z, n)).astype(low)
    input_grad = in_order(ends_line.blocks(), z, n)
    memory_grad = memory_line.total()

    self_tab = table_gradient(self_lines, False, buckets)
    cross_tab = table_gradient(cross_lines, True, buckets)
    spots = [(z + d) % n for d in range(n)]
    tabs = jnp.zeros((2, n, buckets * heads), jnp.float32)
    tabs = lax.dynamic_update_slice(tabs, self_tab.reshape(1, 1, -1), (0, z, 0))
    for d in range(n):
        tabs = lax.dynamic_update_slice(
            tabs, cross_tab[:, d * heads:(d + 1) * heads].reshape(1, 1, -1), (1, spots[d], 0)
        )
    small = jnp.stack([grad_gain_self, grad_gain_cross, grad_gain_ffn, jnp.pad(tabs.reshape(-1), (0, width - tabs.size))], axis=1)
    small = jnp.pad(small, ((0, 0), (0, 124)))
    sums = jnp.concatenate(
        [
            mm(branch_cross, mixed_cross, T0),
            mm(cross_in, cq_grad, T0),
            mm(flat_mem, ckv_grad.reshape(-1, flat_mem.shape[0]), T0),
            mm(branch_self, mixed_self, T0),
            mm(attn_in, sq_grad, T0),
            mm(attn_in, skv_grad, T0),
            small,
        ],
        axis=1,
    )
    sums = lax.psum_scatter(sums, "batch", tiled=True)
    self_sums, small = sums[:, 4 * width:-128], sums[:, -128:]
    attn_line = Scatter(
        [
            jnp.concatenate(
                [sums[:, at * width + d * size:at * width + (d + 1) * size]
                 for at, size in enumerate((ocols, qcols, 2 * kcols, ocols))] + [small],
                axis=1,
            )
            for d in range(n)
        ],
        n,
    )
    attn_line.hop(tie, *one_hop)
    attn_line.hop(tie)
    attn_line.hop(tie)
    attn_sums = attn_line.total()
    ffn_sums = ffn_sums[:3] + lax.ppermute(tie(ffn_sums[3:], sq_grad), "kv", far_pairs)
    ffn_sums = lax.all_gather(tie(ffn_sums, last), "batch", axis=1, tiled=True)
    attn_sums = lax.all_gather(tie(jnp.concatenate([attn_sums, self_sums], axis=1), *memory_three), "batch", tiled=True)

    def columns(x, sizes):
        at = 0
        for size in sizes:
            yield x[:, at:at + size]
            at += size

    grad_co, grad_cq, grad_ck, grad_cv, grad_so, small, grad_sq, grad_sk, grad_sv = columns(
        attn_sums,
        (ocols, qcols, kcols, kcols, ocols, 128, self_query.shape[1], self_key.shape[1], self_value.shape[1]),
    )
    small = small[:, :4].T
    tabs = small[3, :tabs.size].reshape(tabs.shape)
    tabs = lax.dynamic_index_in_dim(tabs, z, 1, keepdims=False).reshape(2, buckets, heads)
    return (
        layer_out.reshape(inputs.shape),
        input_grad.reshape(inputs.shape),
        memory_grad.reshape(1, memory.shape[1], width // n),
        small[0],
        grad_sq,
        grad_sk,
        grad_sv,
        grad_so.T,
        tabs[0],
        small[1],
        grad_cq,
        grad_ck,
        grad_cv,
        grad_co.T,
        tabs[1],
        small[2],
        ffn_sums[0].T,
        ffn_sums[1].T,
        ffn_sums[2],
    )


def solution(mesh):
    return jax.shard_map(
        on_device,
        mesh=mesh,
        in_specs=(
            P("batch", None, None),
            P("batch", None, None),
            P("batch", None, None),
            P(),
            P(None, "kv"),
            P(None, "kv"),
            P(None, "kv"),
            P("kv", None),
            P(None, "kv"),
            P(),
            P(None, "kv"),
            P(None, "kv"),
            P(None, "kv"),
            P("kv", None),
            P(None, "kv"),
            P(),
            P(None, "kv"),
            P(None, "kv"),
            P("kv", None),
        ),
        out_specs=(
            P("batch", None, None),
            P("batch", None, None),
            P("batch", None, "kv"),
            P(),
            P(None, "kv"),
            P(None, "kv"),
            P(None, "kv"),
            P("kv", None),
            P(None, "kv"),
            P(),
            P(None, "kv"),
            P(None, "kv"),
            P(None, "kv"),
            P("kv", None),
            P(None, "kv"),
            P(),
            P(None, "kv"),
            P(None, "kv"),
            P("kv", None),
        ),
        check_vma=False,
    )
```

```python
import functools
import jax, jax.numpy as jnp
import numpy as np
from jax import lax
from jax.experimental import pallas as pl
from jax.experimental.pallas import tpu as pltpu
from jax.sharding import PartitionSpec as P

DH = 64
eps = 1e-06
QB = 256
NEG = -1e30


def cost(scores, weight):
    return pl.CostEstimate(flops=0, transcendentals=0, bytes_accessed=scores * weight)


def mm(a, b, dims):
    return lax.dot_general(a, b, (dims, ((), ())), preferred_element_type=jnp.float32)


NN = ((1,), (0,))
NT = ((1,), (1,))
TN = ((0,), (0,))


def make_band(x_ref, head, band_ref):
    tiles = []
    for d in range(3):
        row = jnp.broadcast_to(x_ref[0, 3 * head + d, :].reshape(1, 256), (128, 256))
        tiles.append(pltpu.roll(row, 0, axis=1, stride=1, stride_axis=0)[:, :128])
    left = jnp.broadcast_to(x_ref[0, 6 + head, 0:128].reshape(1, 128), (128, 128))
    right = jnp.broadcast_to(x_ref[0, 6 + head, 128:256].reshape(1, 128), (128, 128))
    rows = [
        (left, left), (left, left), (left, left),
        (tiles[0], left), (tiles[1], tiles[0]), (tiles[2], tiles[1]), (right, tiles[2]),
        (right, right), (right, right), (right, right),
    ]
    for n, (a, b) in enumerate(rows):
        band_ref[head, n * 128:(n + 1) * 128, 0:128] = a
        band_ref[head, n * 128:(n + 1) * 128, 128:256] = b


def band_at(chunk, block):
    return pl.multiple_of((jnp.clip(chunk - block, -2, 2) + 2) * QB, QB)


def over_chunks(count, body, init):
    if isinstance(count, int):
        for c in range(count):
            init = body(c, init)
        return init
    return lax.fori_loop(0, count, body, init)


def ds(c):
    return pl.ds(pl.multiple_of(c * QB, QB), QB)


def part_sum(tile, op):
    return op(tile.reshape(QB // 8, 8, QB), axis=0)


def fwd_kernel(causal, row_ref, x_ref, q_ref, k_ref, v_ref, o_ref, l_ref, band, keys, s_ref):
    r = pl.program_id(1)
    block = r + row_ref[0]
    total_chunks = k_ref.shape[1] // QB

    @pl.when(r == 0)
    def _():
        for h in range(2):
            make_band(x_ref, h, band)
        keys[...] = k_ref[...].T

    count = block + 1 if causal else total_chunks
    for h in range(2):
        q = q_ref[h * DH:(h + 1) * DH, :]

        def scores(c, top):
            s = mm(keys[ds(c), :], q, NN) + band[h, pl.ds(band_at(c, block), QB), :]
            s_ref[ds(c), :] = s
            return jnp.maximum(top, part_sum(s, jnp.max))

        top = over_chunks(count, scores, jnp.full((8, QB), NEG, jnp.float32))
        top = jnp.max(top, axis=0, keepdims=True)

        def weigh(c, tot):
            e = jnp.exp(s_ref[ds(c), :] - top)
            s_ref[ds(c), :] = e
            return tot + part_sum(e, jnp.sum)

        tot = over_chunks(count, weigh, jnp.zeros((8, QB), jnp.float32))
        tot = jnp.sum(tot, axis=0, keepdims=True)
        inv = 1.0 / tot

        def mix(c, acc):
            p = (s_ref[ds(c), :] * inv).astype(jnp.bfloat16)
            return acc + mm(v_ref[:, ds(c)], p, NN)

        acc = over_chunks(count, mix, jnp.zeros((DH, QB), jnp.float32))
        o_ref[h * DH:(h + 1) * DH, :] = acc.astype(jnp.bfloat16)
        l_ref[0, h:h + 1, :] = top + jnp.log(tot)


def bwd_kernel(causal, row_ref, x_ref, q_ref, k_ref, v_ref, d_ref, l_ref,
               dq_ref, dkv_ref, t_ref, band, keys, values, p_ref, g_ref, near, dk_ref, dv_ref):
    r = pl.program_id(1)
    block = r + row_ref[0]
    total_chunks = k_ref.shape[1] // QB

    @pl.when(r == 0)
    def _():
        for h in range(2):
            make_band(x_ref, h, band)
        keys[...] = k_ref[...].T
        values[...] = v_ref[...].T
        dk_ref[...] = jnp.zeros_like(dk_ref)
        dv_ref[...] = jnp.zeros_like(dv_ref)
        near[...] = jnp.zeros_like(near)

    count = block + 1 if causal else total_chunks
    for h in range(2):
        q = q_ref[h * DH:(h + 1) * DH, :]
        d = d_ref[h * DH:(h + 1) * DH, :]
        log_total = l_ref[0, h:h + 1, :]

        def weigh(c, dot):
            s = mm(keys[ds(c), :], q, NN) + band[h, pl.ds(band_at(c, block), QB), :]
            p = jnp.exp(s - log_total)
            dp = mm(values[ds(c), :], d, NN)
            p_ref[ds(c), :] = p
            g_ref[ds(c), :] = dp
            return dot + part_sum(p * dp, jnp.sum)

        dot = over_chunks(count, weigh, jnp.zeros((8, QB), jnp.float32))
        dot = jnp.sum(dot, axis=0, keepdims=True)

        def back(c, acc):
            p = p_ref[ds(c), :]
            low = (p * (g_ref[ds(c), :] - dot)).astype(jnp.bfloat16)
            dk_ref[:, ds(c)] += mm(q, low, NT)
            dv_ref[:, ds(c)] += mm(d, p.astype(jnp.bfloat16), NT)
            at = pl.ds(band_at(c, block), QB)
            near[h, at, :] += low.astype(jnp.float32)
            return acc + mm(k_ref[:, ds(c)], low, NN)

        acc = over_chunks(count, back, jnp.zeros((DH, QB), jnp.float32))
        dq_ref[h * DH:(h + 1) * DH, :] = acc.astype(jnp.bfloat16)

    @pl.when(r == pl.num_programs(1) - 1)
    def _():
        dkv_ref[0, 0, 0] = dk_ref[...].astype(jnp.bfloat16)
        dkv_ref[0, 1, 0] = dv_ref[...].astype(jnp.bfloat16)
        for h in range(2):
            def piece(n, side):
                return near[h, n * 128:(n + 1) * 128, side * 128:(side + 1) * 128]

            left = piece(3, 1) + sum(piece(n, 0) + piece(n, 1) for n in range(3))
            right = piece(6, 0) + sum(piece(n, 0) + piece(n, 1) for n in range(7, 10))
            tiles = [piece(3, 0) + piece(4, 1), piece(4, 0) + piece(5, 1), piece(5, 0) + piece(6, 1)]
            for n, tile in enumerate(tiles):
                wide = jnp.concatenate([tile, jnp.zeros_like(tile)], axis=1)
                rows = wide[0:8]
                for a in range(8, 128, 8):
                    rows = rows + pltpu.roll(wide[a:a + 8], 256 - a, axis=1)
                line = rows[0:1]
                for b in range(1, 8):
                    line = line + pltpu.roll(rows[b:b + 1], 256 - b, axis=1)
                t_ref[0, 5 * h + n:5 * h + n + 1, :] = line
            for n, far in enumerate((left, right)):
                t_ref[0, 5 * h + 3 + n:5 * h + 4 + n, 0:128] = jnp.sum(far, axis=0, keepdims=True)
                t_ref[0, 5 * h + 3 + n:5 * h + 4 + n, 128:256] = jnp.zeros((1, 128), jnp.float32)


def specs(rows, keys):
    smem = pl.BlockSpec(memory_space=pltpu.SMEM)
    return dict(
        smem=smem,
        x=pl.BlockSpec((1, 8, 256), lambda g, r: (g, 0, 0)),
        q=pl.BlockSpec((2 * DH, QB), lambda g, r: (g, r)),
        k=pl.BlockSpec((DH, keys), lambda g, r: (4 * (g // 2) + g % 2, 0)),
        v=pl.BlockSpec((DH, keys), lambda g, r: (4 * (g // 2) + g % 2 + 2, 0)),
        l=pl.BlockSpec((1, 2, QB), lambda g, r: (g, 0, r)),
        t=pl.BlockSpec((1, 10, 256), lambda g, r: (g, 0, 0)),
    )


def attend(row, x, q, kv, causal):
    groups, keys, rows = kv.shape[0] // (2 * DH), kv.shape[1], q.shape[1]
    s = specs(rows, keys)
    return pl.pallas_call(
        functools.partial(fwd_kernel, causal),
        out_shape=(jax.ShapeDtypeStruct(q.shape, jnp.bfloat16),
                   jax.ShapeDtypeStruct((groups, 2, rows), jnp.float32)),
        grid=(groups, rows // QB),
        in_specs=[s["smem"], s["x"], s["q"], s["k"], s["v"]],
        out_specs=(s["q"], s["l"]),
        scratch_shapes=[pltpu.VMEM((2, 10 * 128, 256), jnp.float32), pltpu.VMEM((keys, DH), jnp.bfloat16),
                        pltpu.VMEM((keys, QB), jnp.float32)],
        compiler_params=pltpu.CompilerParams(dimension_semantics=("arbitrary", "arbitrary"), vmem_limit_bytes=24 << 20),
        cost_estimate=cost(2 * groups * rows * keys, 11),
        name="attend",
    )(row, x, q, kv, kv)


def attend_back(row, x, q, kv, d, logs, causal):
    groups, keys, rows = kv.shape[0] // (2 * DH), kv.shape[1], q.shape[1]
    s = specs(rows, keys)
    dq, dkv, lines = pl.pallas_call(
        functools.partial(bwd_kernel, causal),
        out_shape=[jax.ShapeDtypeStruct(q.shape, jnp.bfloat16),
                   jax.ShapeDtypeStruct((groups // 2, 2, 2, DH, keys), jnp.bfloat16),
                   jax.ShapeDtypeStruct((groups, 10, 256), jnp.float32)],
        grid=(groups, rows // QB),
        in_specs=[s["smem"], s["x"], s["q"], s["k"], s["v"], s["q"], s["l"]],
        out_specs=[s["q"], pl.BlockSpec((1, 2, 1, DH, keys), lambda g, r: (g // 2, 0, g % 2, 0, 0)), s["t"]],
        scratch_shapes=[pltpu.VMEM((2, 10 * 128, 256), jnp.float32), pltpu.VMEM((keys, DH), jnp.bfloat16),
                        pltpu.VMEM((keys, DH), jnp.bfloat16),
                        pltpu.VMEM((keys, QB), jnp.float32), pltpu.VMEM((keys, QB), jnp.float32),
                        pltpu.VMEM((2, 10 * 128, 256), jnp.float32),
                        pltpu.VMEM((DH, keys), jnp.float32), pltpu.VMEM((DH, keys), jnp.float32)],
        compiler_params=pltpu.CompilerParams(dimension_semantics=("arbitrary", "arbitrary"), vmem_limit_bytes=32 << 20),
        cost_estimate=cost(2 * groups * rows * keys, 18),
        name="attend_back",
    )(row, x, q, kv, kv, d, logs)
    return dq, dkv.reshape(kv.shape), lines


MAXDIST = 128


def side_buckets(n, buckets):
    exact = buckets // 2
    scaled = np.log(np.maximum(n, 1) / exact) / np.log(MAXDIST / exact)
    far = np.minimum(exact + np.floor(scaled * (buckets - exact)).astype(np.int64), buckets - 1)
    return np.where(n < exact, n, far)


def relative_buckets(r, two_sided, buckets):
    if two_sided:
        per = buckets // 2
        return side_buckets(np.abs(r), per) + np.where(r > 0, per, 0)
    return side_buckets(np.maximum(-r, 0), buckets)


def lane_offsets():
    m = np.arange(256)
    return np.stack([128 * d - np.where(m < 128, m, m - 256) for d in (-1, 0, 1)])


def bias_vectors(table, two_sided):
    buckets, heads = table.shape
    rel = lane_offsets()
    ids = relative_buckets(rel, two_sided, buckets)
    onehot = (ids.reshape(-1)[:, None] == np.arange(buckets)[None, :])
    x = jnp.dot(jnp.asarray(onehot, jnp.bfloat16), table, preferred_element_type=jnp.float32)
    x = x.reshape(3, 256, heads)
    last = table.shape[0] - 1
    if two_sided:
        left, right = table[last // 2].astype(jnp.float32), table[last].astype(jnp.float32)
    else:
        x = jnp.where(jnp.asarray(rel > 0)[:, :, None], NEG, x)
        left, right = table[last].astype(jnp.float32), jnp.full((heads,), NEG, jnp.float32)
    x = jnp.transpose(x, (2, 0, 1)).reshape(heads // 2, 6, 256)
    far = jnp.stack([left, right], axis=1).reshape(heads // 2, 2, 2, 1)
    return jnp.concatenate([x, jnp.broadcast_to(far, far.shape[:3] + (128,)).reshape(heads // 2, 2, 256)], axis=1)


def table_gradient(t, two_sided, buckets):
    groups = t.shape[0]
    t = t.reshape(2 * groups, 5, 256)
    rel = lane_offsets()
    ids = relative_buckets(rel, two_sided, buckets)
    onehot = np.zeros((5, 256, buckets), np.float32)
    onehot[:3] = (ids[:, :, None] == np.arange(buckets)) & (np.arange(256) != 128)[None, :, None]
    last = buckets - 1
    if two_sided:
        onehot[3, :, last // 2] = 1
        onehot[4, :, last] = 1
    else:
        onehot[:3] *= (rel <= 0)[:, :, None]
        onehot[3, :, last] = 1
    return lax.dot_general(jnp.asarray(onehot.reshape(5 * 256, buckets), jnp.bfloat16).astype(jnp.float32), t.reshape(2 * groups, 5 * 256),
                           (((0,), (1,)), ((), ())), precision=lax.Precision.HIGHEST)


def norm_rows(hidden, gain_vec):
    inv_scale = lax.rsqrt(jnp.mean(hidden * hidden, axis=-1, keepdims=True) + eps)
    return hidden * inv_scale * gain_vec


def gate_times_up(gate_value, up_value):
    return jax.nn.gelu(gate_value, approximate=True) * up_value


T0 = ((0,), (1,))


def block_of(x, index, size, axis=0):
    return lax.dynamic_slice_in_dim(x, index * size, size, axis)


class Gather:
    def __init__(self, x, n):
        self.n, self.x, self.d = n, x, 0
        self.right = self.left = x
        self.from_left, self.from_right = [], []

    def hop(self, tie, *others):
        n, self.d = self.n, self.d + 1
        d = self.d
        self.right = lax.ppermute(tie(self.right, *others), "kv", [(i, i + 1) for i in range(d - 1, n - 1)])
        self.left = lax.ppermute(tie(self.left, *others), "kv", [(i + 1, i) for i in range(n - d)])
        self.from_left.append(self.right)
        self.from_right.append(self.left)
        return [self.right, self.left]

    def blocks(self):
        n = self.n
        return [self.x] + [self.from_right[d - 1] + self.from_left[n - d - 1] for d in range(1, n)]


class Scatter:
    def __init__(self, parts, n):
        self.n, self.parts, self.d = n, parts, n
        self.got = [0.0, 0.0]

    def hop(self, tie, *others):
        n, self.d = self.n, self.d - 1
        d = self.d
        right, left = self.parts[d] + self.got[0], self.parts[n - d] + self.got[1]
        self.got = [
            lax.ppermute(tie(right, *others), "kv", [(i, i + 1) for i in range(n - d)]),
            lax.ppermute(tie(left, *others), "kv", [(i + 1, i) for i in range(d - 1, n - 1)]),
        ]
        return self.got

    def total(self):
        return self.parts[0] + self.got[0] + self.got[1]


def in_order(blocks, z, n):
    stacked = jnp.stack(blocks)
    return jnp.concatenate(
        [lax.dynamic_index_in_dim(stacked, (j - z + n) % n, 0, keepdims=False) for j in range(n)]
    )


def exchange(blocks, n):
    got = [blocks[0]]
    for d in range(1, n):
        got.append(lax.ppermute(blocks[n - d], "kv", [((i + d) % n, i) for i in range(n)]))
    return got


def whole_kernel(thin, deep, shares_ref, in_ref, so_ref, co_ref, *refs):
    so_out, co_out, cq_out, kv_out = refs[-4:]
    d = pl.program_id(0)
    half = shares_ref.shape[3]
    qcols = cq_out.shape[2]

    @pl.when(d == 0)
    def _():
        so_out[...] = so_ref[...]
        co_out[...] = co_ref[...]
        cq_out[0] = in_ref[:, :qcols]
        kv_out[0] = in_ref[:, qcols:]

    @pl.when(d > 0)
    def _():
        for i in range(shares_ref.shape[0]):
            here = shares_ref[i, 0, 0:deep, :].astype(jnp.bfloat16)
            cq_out[0, i * deep:(i + 1) * deep, :] = here[:, :qcols]
            kv_out[0, i * deep:(i + 1) * deep, :] = here[:, qcols:]
            for n, ref in enumerate((so_out, co_out)):
                for side in range(2):
                    at = deep + (2 * n + side) * thin
                    ref[i * thin:(i + 1) * thin, side * half:(side + 1) * half] = (
                        shares_ref[i, 0, at:at + thin, :].astype(jnp.bfloat16)
                    )


def whole_weights(shares, own_in, own_so, own_co, earlier):
    nb, others = shares.shape[:2]
    width, cols = own_in.shape
    tall = own_so.shape[0]
    step = 4
    turns = nb // step
    own = lambda d, i: (jnp.where(d == 0, i, turns - 1), 0)
    flat = pl.BlockSpec((tall // turns, width), lambda d, i: (d * turns + i, 0))
    deep = pl.BlockSpec((1, width // turns, cols // 2), lambda d, i: (d, i, 0))
    return pl.pallas_call(
        functools.partial(whole_kernel, tall // nb, width // nb),
        out_shape=(jax.ShapeDtypeStruct(((others + 1) * tall, width), jnp.bfloat16),) * 2
        + (jax.ShapeDtypeStruct((others + 1, width, cols // 2), jnp.bfloat16),) * 2,
        grid=(others + 1, turns),
        in_specs=[
            pl.BlockSpec((step, 1) + shares.shape[2:], lambda d, i: (jnp.where(d == 0, 0, i), jnp.maximum(d - 1, 0), 0, 0)),
            pl.BlockSpec((width // turns, cols), own),
            pl.BlockSpec((tall // turns, width), own),
            pl.BlockSpec((tall // turns, width), own),
        ] + [pl.BlockSpec((16, 128), lambda d, i: (0, 0))] * len(earlier),
        out_specs=(flat, flat, deep, deep),
        compiler_params=pltpu.CompilerParams(dimension_semantics=("arbitrary", "arbitrary"), vmem_limit_bytes=32 << 20),
        cost_estimate=cost(shares.size, 7),
        name="whole_weights",
    )(shares, own_in, own_so, own_co, *earlier)


def on_device(
    inputs,
    memory,
    out_grad,
    gain_self,
    self_query,
    self_key,
    self_value,
    self_output,
    self_table,
    gain_cross,
    cross_query,
    cross_key,
    cross_value,
    cross_output,
    cross_table,
    gain_ffn,
    ffn_gate,
    ffn_up,
    ffn_down,
):
    seq_len = inputs.shape[1]
    width = inputs.shape[2]
    n, nb = lax.axis_size("kv"), lax.axis_size("batch")
    z, b = lax.axis_index("kv"), lax.axis_index("batch")
    rows = seq_len // n
    low = jnp.bfloat16
    one = jnp.where(gain_self[0] < 100, 1.0, 2.0).astype(jnp.float32)

    def settle(x):
        return x * one

    def tie(x, *others):
        for other in others:
            x = x + other[(0,) * other.ndim].astype(jnp.float32) * (one - 1.0)
        return x

    def share(w):
        return block_of(w, b, w.shape[0] // nb).astype(jnp.float32)

    def halves(x):
        return jnp.concatenate([x[:, :width // 2], x[:, width // 2:]])

    qcols, kcols, ocols = cross_query.shape[1], cross_key.shape[1], cross_output.shape[0]
    far_pairs = [(i, i ^ 2) for i in range(n)]
    near_pairs = [(i, i ^ 1) for i in range(n)]
    cross_kv = jnp.concatenate([cross_key, cross_value], axis=1)
    unit = jnp.concatenate(
        [
            jnp.concatenate([share(cross_query), share(cross_kv)], axis=1),
            halves(share(self_output)),
            halves(share(cross_output)),
        ]
    )
    units = exchange([unit] * n, n)[1:]

    gain_one = gain_self.astype(jnp.float32)
    gain_two = gain_cross.astype(jnp.float32)
    gain_three = gain_ffn.astype(jnp.float32)
    self_x, own_cross_x = bias_vectors(self_table, False), bias_vectors(cross_table, True)

    flat_in = inputs.reshape(seq_len, width).astype(jnp.float32)
    flat_mem = memory.reshape(memory.shape[1], width)
    attn_in = norm_rows(flat_in, gain_one).astype(low)
    zero = jnp.zeros((1,), jnp.int32)
    self_kv = jnp.concatenate([self_key, self_value], axis=1)
    sq = mm(self_query, attn_in, T0).astype(low)
    skv = mm(self_kv, attn_in, T0).astype(low)
    mixed, self_log = attend(zero, self_x, sq, skv, True)
    buckets, heads = self_table.shape
    deep, thin = width // nb, ocols // nb
    shares = lax.all_gather(tie(jnp.stack(units), mixed), "batch")
    mixed = tie(mixed.astype(jnp.float32), *units)
    rider = own_cross_x.reshape(-1, rows)
    own_self = jnp.concatenate([self_query, self_kv], axis=1)
    got = exchange([jnp.concatenate([block_of(mixed, (z + d) % n, rows, 1), rider]) for d in range(n)], n)
    others = got[1:]
    mixed_self = settle(jnp.concatenate([x[:ocols] for x in got])).astype(low)
    ridden = ocols + rider.shape[0]
    cross_x = jnp.concatenate([x[ocols:ridden] for x in got]).reshape(-1, 8, rows)
    own_in = jnp.concatenate([cross_query, cross_kv], axis=1)
    whole_so, whole_co, whole_cq, whole_kv = whole_weights(
        shares, own_in, self_output, cross_output, [mixed_self, cross_x.reshape(-1, rows)]
    )

    sent = jnp.stack([share(ffn_gate.T), share(ffn_up.T), share(ffn_down)])
    fetched = lax.ppermute(tie(sent, *others), "kv", far_pairs)
    sent = lax.all_gather(tie(fetched, whole_so), "batch", axis=1, tiled=True)

    in_rows = block_of(inputs.reshape(seq_len, width), z, rows).astype(jnp.float32)
    after_self = in_rows + mm(mixed_self, whole_so, TN)

    def into(w, x):
        y = lax.dot_general(w, x, (((1,), (1,)), ((), ())), preferred_element_type=jnp.float32)
        return y.astype(low).reshape(-1, x.shape[0])

    ckv = into(whole_kv, flat_mem)
    cross_in = norm_rows(after_self, gain_two).astype(low)
    cq = into(whole_cq, cross_in)
    place = z.reshape(1).astype(jnp.int32) * (rows // QB)
    mixed_cross, cross_log = attend(place, cross_x, cq, ckv, False)
    after_cross = after_self + mm(mixed_cross, whole_co, TN)

    ffn_in = norm_rows(after_cross, gain_three).astype(low)
    other = settle(lax.ppermute(ffn_in.astype(jnp.float32), "kv", near_pairs)).astype(low)
    flat_grad = out_grad.reshape(seq_len, width)
    own_grad = block_of(flat_grad, z, rows)
    far_ffn = settle(sent).astype(low)
    weights = ((ffn_gate, ffn_up, ffn_down, False), (far_ffn[0], far_ffn[1], far_ffn[2], True))
    parts, grads, inputs_of = [], [], ((ffn_in, own_grad), (other, block_of(flat_grad, z ^ 1, rows)))
    for x, dy in inputs_of:
        in_part = out_part = 0.0
        for w_gate, w_up, w_down, turned in weights:
            there, back = (NT, NN) if turned else (NN, NT)
            gate_pre, up_pre = mm(x, w_gate, there), mm(x, w_up, there)
            hidden = gate_times_up(gate_pre, up_pre).astype(low)
            out_part = out_part + mm(hidden, w_down, NN)
            gate_grad, up_grad = jax.vjp(gate_times_up, gate_pre, up_pre)[1](mm(dy, w_down, NT))
            gate_grad, up_grad = gate_grad.astype(low), up_grad.astype(low)
            in_part = in_part + mm(gate_grad, w_gate, back) + mm(up_grad, w_up, back)
            grads.append((gate_grad, up_grad, hidden))
        parts.append((in_part, out_part))
    ffn_in_grad = parts[0][0] + lax.ppermute(parts[1][0], "kv", near_pairs)
    both_in, both_grad = (jnp.concatenate(x) for x in zip(*inputs_of))
    ffn_sums = jnp.stack(
        [
            mm(jnp.concatenate([grads[side][kind], grads[2 + side][kind]]), both_grad if kind == 2 else both_in, TN)
            for side in range(2) for kind in range(3)
        ]
    )
    ffn_sums = lax.psum_scatter(ffn_sums, "batch", scatter_dimension=1, tiled=True)
    ffn_out = parts[0][1] + lax.ppermute(tie(parts[1][1], ffn_in_grad), "kv", near_pairs)

    norm_grad, grad_gain_ffn = jax.vjp(norm_rows, after_cross, gain_three)[1](ffn_in_grad)
    cross_out_grad = own_grad.astype(jnp.float32) + norm_grad
    branch_cross = cross_out_grad.astype(low)
    mixed_grad = mm(whole_co, branch_cross, NT).astype(low)
    cq_grad, ckv_grad, cross_lines = attend_back(
        place, cross_x, cq, ckv, mixed_grad, cross_log, False
    )
    cross_in_grad = lax.dot_general(
        cq_grad.reshape(n, qcols, rows), whole_cq, (((0, 1), (0, 2)), ((), ())), preferred_element_type=jnp.float32
    )
    norm_grad, grad_gain_cross = jax.vjp(norm_rows, after_self, gain_two)[1](cross_in_grad)
    self_out_grad = cross_out_grad + norm_grad
    branch_self = self_out_grad.astype(low)
    mixed_grad = tie(mm(whole_so, branch_self, NT).astype(low).astype(jnp.float32), ffn_out)
    got = exchange([mixed_grad[d * ocols:(d + 1) * ocols] for d in range(n)], n)
    arrived = got[1:]
    stacked = jnp.stack(got)
    mixed_grad = tie(
        jnp.concatenate(
            [lax.dynamic_index_in_dim(stacked, (j - z + n) % n, 0, keepdims=False) for j in range(n)], axis=1
        ),
    )
    mixed_grad = settle(mixed_grad).astype(low)
    memory_part = lax.dot_general(
        ckv_grad.reshape(n, 2 * kcols, -1), whole_kv, (((0, 1), (0, 2)), ((), ())), preferred_element_type=jnp.float32
    )
    memory_grad = lax.psum_scatter(tie(memory_part, *arrived), "kv", scatter_dimension=1, tiled=True)

    arriving = exchange([tie(share(own_self), fetched, after_cross)] * n, n)[1:]
    rest_self = tie(jnp.stack(arriving), cq_grad, ffn_sums)
    rest_self = settle(lax.all_gather(rest_self, "batch", axis=1, tiled=True)).astype(low)

    sq_grad, skv_grad, self_lines = attend_back(zero, self_x, sq, skv, mixed_grad, self_log, True)
    turned = jnp.concatenate([sq_grad, skv_grad]).astype(jnp.float32)
    got = exchange([block_of(turned, (z + d) % n, rows, 1) for d in range(n)], n)
    rest = settle(jnp.stack(got[1:])).astype(low)
    attn_in_grad = mm(got[0].astype(low), own_self, T0) + lax.dot_general(
        rest, rest_self, (((0, 1), (0, 2)), ((), ())), preferred_element_type=jnp.float32
    )
    early = got[1:]
    attn_term = mm(sq_grad, self_query, T0) + mm(skv_grad, self_kv, T0)
    norm_grad, _ = jax.vjp(norm_rows, in_rows, gain_one)[1](attn_in_grad)
    last = self_out_grad + norm_grad
    _, grad_gain_self = jax.vjp(norm_rows, flat_in, gain_one)[1](attn_term)

    result = (tie(after_cross, *early) + ffn_out).astype(low).astype(jnp.float32)
    line = Gather(result, n)
    ends_line = Gather(last, n)
    one_hop = ends_line.hop(tie)
    two_hops = ends_line.hop(tie)
    three_hops = ends_line.hop(tie)
    line.hop(tie)
    lo_two = line.hop(tie)
    line.hop(tie)
    layer_out = settle(in_order(line.blocks(), z, n)).astype(low)
    input_grad = in_order(ends_line.blocks(), z, n)

    self_tab = table_gradient(self_lines, False, buckets)
    cross_tab = table_gradient(cross_lines, True, buckets)
    spots = [(z + d) % n for d in range(n)]
    tabs = jnp.zeros((2, n, buckets * heads), jnp.float32)
    tabs = lax.dynamic_update_slice(tabs, self_tab.reshape(1, 1, -1), (0, z, 0))
    for d in range(n):
        tabs = lax.dynamic_update_slice(
            tabs, cross_tab[:, d * heads:(d + 1) * heads].reshape(1, 1, -1), (1, spots[d], 0)
        )
    small = jnp.stack([grad_gain_self, grad_gain_cross, grad_gain_ffn, jnp.pad(tabs.reshape(-1), (0, width - tabs.size))], axis=1)
    small = jnp.pad(tie(small, *early), ((0, 0), (0, 124)))
    sums = jnp.concatenate(
        [
            mm(branch_cross, mixed_cross, T0),
            mm(cross_in, cq_grad, T0),
            mm(flat_mem, ckv_grad, T0),
            mm(branch_self, mixed_self, T0),
            mm(attn_in, sq_grad, T0),
            mm(attn_in, skv_grad, T0),
            small,
        ],
        axis=1,
    )
    sums = lax.psum_scatter(sums, "batch", tiled=True)
    self_sums, small = sums[:, 4 * width:-128], sums[:, -128:]
    parts = [
        jnp.concatenate(
            [sums[:, at * width + d * size:at * width + (d + 1) * size]
             for at, size in enumerate((ocols, qcols, 2 * kcols, ocols))] + [small],
            axis=1,
        )
        for d in range(n)
    ]
    attn_sums = sum(exchange([tie(x, *three_hops) for x in parts], n))
    ffn_sums = ffn_sums[:3] + lax.ppermute(tie(ffn_sums[3:], *arrived), "kv", far_pairs)
    ffn_sums = lax.all_gather(tie(ffn_sums, last, memory_grad), "batch", axis=1, tiled=True)
    attn_sums = lax.all_gather(tie(jnp.concatenate([attn_sums, self_sums], axis=1), *lo_two), "batch", tiled=True)

    def columns(x, sizes):
        at = 0
        for size in sizes:
            yield x[:, at:at + size]
            at += size

    grad_co, grad_cq, grad_ck, grad_cv, grad_so, small, grad_sq, grad_sk, grad_sv = columns(
        attn_sums,
        (ocols, qcols, kcols, kcols, ocols, 128, self_query.shape[1], self_key.shape[1], self_value.shape[1]),
    )
    small = small[:, :4].T
    tabs = small[3, :tabs.size].reshape(tabs.shape)
    tabs = lax.dynamic_index_in_dim(tabs, z, 1, keepdims=False).reshape(2, buckets, heads)
    return (
        layer_out.reshape(inputs.shape),
        input_grad.reshape(inputs.shape),
        memory_grad.reshape(1, memory.shape[1], width // n),
        small[0],
        grad_sq,
        grad_sk,
        grad_sv,
        grad_so.T,
        tabs[0],
        small[1],
        grad_cq,
        grad_ck,
        grad_cv,
        grad_co.T,
        tabs[1],
        small[2],
        ffn_sums[0].T,
        ffn_sums[1].T,
        ffn_sums[2],
    )


def solution(mesh):
    return jax.shard_map(
        on_device,
        mesh=mesh,
        in_specs=(
            P("batch", None, None),
            P("batch", None, None),
            P("batch", None, None),
            P(),
            P(None, "kv"),
            P(None, "kv"),
            P(None, "kv"),
            P("kv", None),
            P(None, "kv"),
            P(),
            P(None, "kv"),
            P(None, "kv"),
            P(None, "kv"),
            P("kv", None),
            P(None, "kv"),
            P(),
            P(None, "kv"),
            P(None, "kv"),
            P("kv", None),
        ),
        out_specs=(
            P("batch", None, None),
            P("batch", None, None),
            P("batch", None, "kv"),
            P(),
            P(None, "kv"),
            P(None, "kv"),
            P(None, "kv"),
            P("kv", None),
            P(None, "kv"),
            P(),
            P(None, "kv"),
            P(None, "kv"),
            P(None, "kv"),
            P("kv", None),
            P(None, "kv"),
            P(),
            P(None, "kv"),
            P(None, "kv"),
            P("kv", None),
        ),
        check_vma=False,
    )
```

```python
import functools
import jax, jax.numpy as jnp
import numpy as np
from jax import lax
from jax.experimental import pallas as pl
from jax.experimental.pallas import tpu as pltpu
from jax.sharding import PartitionSpec as P

DH = 64
eps = 1e-06
QB = 256
NEG = -1e30


def cost(scores, weight):
    return pl.CostEstimate(flops=0, transcendentals=0, bytes_accessed=scores * weight)


def mm(a, b, dims):
    return lax.dot_general(a, b, (dims, ((), ())), preferred_element_type=jnp.float32)


NN = ((1,), (0,))
NT = ((1,), (1,))
TN = ((0,), (0,))


def make_band(x_ref, head, band_ref):
    tiles = []
    for d in range(3):
        row = jnp.broadcast_to(x_ref[0, 3 * head + d, :].reshape(1, 256), (128, 256))
        tiles.append(pltpu.roll(row, 0, axis=1, stride=1, stride_axis=0)[:, :128])
    left = jnp.broadcast_to(x_ref[0, 6 + head, 0:128].reshape(1, 128), (128, 128))
    right = jnp.broadcast_to(x_ref[0, 6 + head, 128:256].reshape(1, 128), (128, 128))
    rows = [
        (left, left), (left, left), (left, left),
        (tiles[0], left), (tiles[1], tiles[0]), (tiles[2], tiles[1]), (right, tiles[2]),
        (right, right), (right, right), (right, right),
    ]
    for n, (a, b) in enumerate(rows):
        band_ref[head, n * 128:(n + 1) * 128, 0:128] = a
        band_ref[head, n * 128:(n + 1) * 128, 128:256] = b


def band_at(chunk, block):
    return pl.multiple_of((jnp.clip(chunk - block, -2, 2) + 2) * QB, QB)


def over_chunks(count, body, init):
    for c in range(count):
        init = body(c, init)
    return init


def by_length(causal, block, total_chunks, work):
    if not causal:
        work(total_chunks)
        return
    for k in range(total_chunks):
        pl.when(block == k)(functools.partial(work, k + 1))


def ds(c):
    return pl.ds(pl.multiple_of(c * QB, QB), QB)


def part_sum(tile, op):
    return op(tile.reshape(QB // 8, 8, QB), axis=0)


def fwd_kernel(causal, row_ref, x_ref, q_ref, k_ref, v_ref, o_ref, l_ref, band, keys, s_ref):
    r = pl.program_id(1)
    block = r + row_ref[0]
    total_chunks = k_ref.shape[1] // QB

    @pl.when(r == 0)
    def _():
        for h in range(2):
            make_band(x_ref, h, band)
        keys[...] = k_ref[...].T

    def work(count):
        for h in range(2):
            q = q_ref[h * DH:(h + 1) * DH, :]

            def scores(c, top):
                s = mm(keys[ds(c), :], q, NN) + band[h, pl.ds(band_at(c, block), QB), :]
                s_ref[ds(c), :] = s
                return jnp.maximum(top, part_sum(s, jnp.max))

            top = over_chunks(count, scores, jnp.full((8, QB), NEG, jnp.float32))
            top = jnp.max(top, axis=0, keepdims=True)

            def weigh(c, tot):
                e = jnp.exp(s_ref[ds(c), :] - top)
                s_ref[ds(c), :] = e
                return tot + part_sum(e, jnp.sum)

            tot = over_chunks(count, weigh, jnp.zeros((8, QB), jnp.float32))
            tot = jnp.sum(tot, axis=0, keepdims=True)
            inv = 1.0 / tot

            def mix(c, acc):
                p = (s_ref[ds(c), :] * inv).astype(jnp.bfloat16)
                return acc + mm(v_ref[:, ds(c)], p, NN)

            acc = over_chunks(count, mix, jnp.zeros((DH, QB), jnp.float32))
            o_ref[h * DH:(h + 1) * DH, :] = acc.astype(jnp.bfloat16)
            l_ref[0, h:h + 1, :] = top + jnp.log(tot)

    by_length(causal, block, total_chunks, work)


def bwd_kernel(causal, row_ref, x_ref, q_ref, k_ref, v_ref, d_ref, l_ref,
               dq_ref, dkv_ref, t_ref, band, keys, values, p_ref, g_ref, near, dk_ref, dv_ref):
    r = pl.program_id(1)
    block = r + row_ref[0]
    total_chunks = k_ref.shape[1] // QB

    @pl.when(r == 0)
    def _():
        for h in range(2):
            make_band(x_ref, h, band)
        keys[...] = k_ref[...].T
        values[...] = v_ref[...].T
        dk_ref[...] = jnp.zeros_like(dk_ref)
        dv_ref[...] = jnp.zeros_like(dv_ref)
        near[...] = jnp.zeros_like(near)

    def work(count):
        for h in range(2):
            q = q_ref[h * DH:(h + 1) * DH, :]
            d = d_ref[h * DH:(h + 1) * DH, :]
            log_total = l_ref[0, h:h + 1, :]

            def weigh(c, dot):
                s = mm(keys[ds(c), :], q, NN) + band[h, pl.ds(band_at(c, block), QB), :]
                p = jnp.exp(s - log_total)
                dp = mm(values[ds(c), :], d, NN)
                p_ref[ds(c), :] = p
                g_ref[ds(c), :] = dp
                return dot + part_sum(p * dp, jnp.sum)

            dot = over_chunks(count, weigh, jnp.zeros((8, QB), jnp.float32))
            dot = jnp.sum(dot, axis=0, keepdims=True)

            def back(c, acc):
                p = p_ref[ds(c), :]
                low = (p * (g_ref[ds(c), :] - dot)).astype(jnp.bfloat16)
                dk_ref[:, ds(c)] += mm(q, low, NT)
                dv_ref[:, ds(c)] += mm(d, p.astype(jnp.bfloat16), NT)
                at = pl.ds(band_at(c, block), QB)
                near[h, at, :] += low.astype(jnp.float32)
                return acc + mm(k_ref[:, ds(c)], low, NN)

            acc = over_chunks(count, back, jnp.zeros((DH, QB), jnp.float32))
            dq_ref[h * DH:(h + 1) * DH, :] = acc.astype(jnp.bfloat16)

    by_length(causal, block, total_chunks, work)

    @pl.when(r == pl.num_programs(1) - 1)
    def _():
        dkv_ref[0, 0, 0] = dk_ref[...].astype(jnp.bfloat16)
        dkv_ref[0, 1, 0] = dv_ref[...].astype(jnp.bfloat16)
        for h in range(2):
            def piece(n, side):
                return near[h, n * 128:(n + 1) * 128, side * 128:(side + 1) * 128]

            left = piece(3, 1) + sum(piece(n, 0) + piece(n, 1) for n in range(3))
            right = piece(6, 0) + sum(piece(n, 0) + piece(n, 1) for n in range(7, 10))
            tiles = [piece(3, 0) + piece(4, 1), piece(4, 0) + piece(5, 1), piece(5, 0) + piece(6, 1)]
            for n, tile in enumerate(tiles):
                wide = jnp.concatenate([tile, jnp.zeros_like(tile)], axis=1)
                rows = wide[0:8]
                for a in range(8, 128, 8):
                    rows = rows + pltpu.roll(wide[a:a + 8], 256 - a, axis=1)
                line = rows[0:1]
                for b in range(1, 8):
                    line = line + pltpu.roll(rows[b:b + 1], 256 - b, axis=1)
                t_ref[0, 5 * h + n:5 * h + n + 1, :] = line
            for n, far in enumerate((left, right)):
                t_ref[0, 5 * h + 3 + n:5 * h + 4 + n, 0:128] = jnp.sum(far, axis=0, keepdims=True)
                t_ref[0, 5 * h + 3 + n:5 * h + 4 + n, 128:256] = jnp.zeros((1, 128), jnp.float32)


def specs(rows, keys):
    smem = pl.BlockSpec(memory_space=pltpu.SMEM)
    return dict(
        smem=smem,
        x=pl.BlockSpec((1, 8, 256), lambda g, r: (g, 0, 0)),
        q=pl.BlockSpec((2 * DH, QB), lambda g, r: (g, r)),
        k=pl.BlockSpec((DH, keys), lambda g, r: (4 * (g // 2) + g % 2, 0)),
        v=pl.BlockSpec((DH, keys), lambda g, r: (4 * (g // 2) + g % 2 + 2, 0)),
        l=pl.BlockSpec((1, 2, QB), lambda g, r: (g, 0, r)),
        t=pl.BlockSpec((1, 10, 256), lambda g, r: (g, 0, 0)),
    )


def attend(row, x, q, kv, causal):
    groups, keys, rows = kv.shape[0] // (2 * DH), kv.shape[1], q.shape[1]
    s = specs(rows, keys)
    return pl.pallas_call(
        functools.partial(fwd_kernel, causal),
        out_shape=(jax.ShapeDtypeStruct(q.shape, jnp.bfloat16),
                   jax.ShapeDtypeStruct((groups, 2, rows), jnp.float32)),
        grid=(groups, rows // QB),
        in_specs=[s["smem"], s["x"], s["q"], s["k"], s["v"]],
        out_specs=(s["q"], s["l"]),
        scratch_shapes=[pltpu.VMEM((2, 10 * 128, 256), jnp.float32), pltpu.VMEM((keys, DH), jnp.bfloat16),
                        pltpu.VMEM((keys, QB), jnp.float32)],
        compiler_params=pltpu.CompilerParams(dimension_semantics=("arbitrary", "arbitrary"), vmem_limit_bytes=24 << 20),
        cost_estimate=cost(2 * groups * rows * keys, 11),
        name="attend",
    )(row, x, q, kv, kv)


def attend_back(row, x, q, kv, d, logs, causal):
    groups, keys, rows = kv.shape[0] // (2 * DH), kv.shape[1], q.shape[1]
    s = specs(rows, keys)
    dq, dkv, lines = pl.pallas_call(
        functools.partial(bwd_kernel, causal),
        out_shape=[jax.ShapeDtypeStruct(q.shape, jnp.bfloat16),
                   jax.ShapeDtypeStruct((groups // 2, 2, 2, DH, keys), jnp.bfloat16),
                   jax.ShapeDtypeStruct((groups, 10, 256), jnp.float32)],
        grid=(groups, rows // QB),
        in_specs=[s["smem"], s["x"], s["q"], s["k"], s["v"], s["q"], s["l"]],
        out_specs=[s["q"], pl.BlockSpec((1, 2, 1, DH, keys), lambda g, r: (g // 2, 0, g % 2, 0, 0)), s["t"]],
        scratch_shapes=[pltpu.VMEM((2, 10 * 128, 256), jnp.float32), pltpu.VMEM((keys, DH), jnp.bfloat16),
                        pltpu.VMEM((keys, DH), jnp.bfloat16),
                        pltpu.VMEM((keys, QB), jnp.float32), pltpu.VMEM((keys, QB), jnp.float32),
                        pltpu.VMEM((2, 10 * 128, 256), jnp.float32),
                        pltpu.VMEM((DH, keys), jnp.float32), pltpu.VMEM((DH, keys), jnp.float32)],
        compiler_params=pltpu.CompilerParams(dimension_semantics=("arbitrary", "arbitrary"), vmem_limit_bytes=32 << 20),
        cost_estimate=cost(2 * groups * rows * keys, 18),
        name="attend_back",
    )(row, x, q, kv, kv, d, logs)
    return dq, dkv.reshape(kv.shape), lines


MAXDIST = 128


def side_buckets(n, buckets):
    exact = buckets // 2
    scaled = np.log(np.maximum(n, 1) / exact) / np.log(MAXDIST / exact)
    far = np.minimum(exact + np.floor(scaled * (buckets - exact)).astype(np.int64), buckets - 1)
    return np.where(n < exact, n, far)


def relative_buckets(r, two_sided, buckets):
    if two_sided:
        per = buckets // 2
        return side_buckets(np.abs(r), per) + np.where(r > 0, per, 0)
    return side_buckets(np.maximum(-r, 0), buckets)


def lane_offsets():
    m = np.arange(256)
    return np.stack([128 * d - np.where(m < 128, m, m - 256) for d in (-1, 0, 1)])


def bias_vectors(table, two_sided):
    buckets, heads = table.shape
    rel = lane_offsets()
    ids = relative_buckets(rel, two_sided, buckets)
    onehot = (ids.reshape(-1)[:, None] == np.arange(buckets)[None, :])
    x = jnp.dot(jnp.asarray(onehot, jnp.bfloat16), table, preferred_element_type=jnp.float32)
    x = x.reshape(3, 256, heads)
    last = table.shape[0] - 1
    if two_sided:
        left, right = table[last // 2].astype(jnp.float32), table[last].astype(jnp.float32)
    else:
        x = jnp.where(jnp.asarray(rel > 0)[:, :, None], NEG, x)
        left, right = table[last].astype(jnp.float32), jnp.full((heads,), NEG, jnp.float32)
    x = jnp.transpose(x, (2, 0, 1)).reshape(heads // 2, 6, 256)
    far = jnp.stack([left, right], axis=1).reshape(heads // 2, 2, 2, 1)
    return jnp.concatenate([x, jnp.broadcast_to(far, far.shape[:3] + (128,)).reshape(heads // 2, 2, 256)], axis=1)


def table_gradient(t, two_sided, buckets):
    groups = t.shape[0]
    t = t.reshape(2 * groups, 5, 256)
    rel = lane_offsets()
    ids = relative_buckets(rel, two_sided, buckets)
    onehot = np.zeros((5, 256, buckets), np.float32)
    onehot[:3] = (ids[:, :, None] == np.arange(buckets)) & (np.arange(256) != 128)[None, :, None]
    last = buckets - 1
    if two_sided:
        onehot[3, :, last // 2] = 1
        onehot[4, :, last] = 1
    else:
        onehot[:3] *= (rel <= 0)[:, :, None]
        onehot[3, :, last] = 1
    return lax.dot_general(jnp.asarray(onehot.reshape(5 * 256, buckets), jnp.bfloat16).astype(jnp.float32), t.reshape(2 * groups, 5 * 256),
                           (((0,), (1,)), ((), ())), precision=lax.Precision.HIGHEST)


def norm_rows(hidden, gain_vec):
    inv_scale = lax.rsqrt(jnp.mean(hidden * hidden, axis=-1, keepdims=True) + eps)
    return hidden * inv_scale * gain_vec


def gate_times_up(gate_value, up_value):
    return jax.nn.gelu(gate_value, approximate=True) * up_value


T0 = ((0,), (1,))


def block_of(x, index, size, axis=0):
    return lax.dynamic_slice_in_dim(x, index * size, size, axis)


class Gather:
    def __init__(self, x, n):
        self.n, self.x, self.d = n, x, 0
        self.right = self.left = x
        self.from_left, self.from_right = [], []

    def hop(self, tie, *others):
        n, self.d = self.n, self.d + 1
        d = self.d
        self.right = lax.ppermute(tie(self.right, *others), "kv", [(i, i + 1) for i in range(d - 1, n - 1)])
        self.left = lax.ppermute(tie(self.left, *others), "kv", [(i + 1, i) for i in range(n - d)])
        self.from_left.append(self.right)
        self.from_right.append(self.left)
        return [self.right, self.left]

    def blocks(self):
        n = self.n
        return [self.x] + [self.from_right[d - 1] + self.from_left[n - d - 1] for d in range(1, n)]


class Scatter:
    def __init__(self, parts, n):
        self.n, self.parts, self.d = n, parts, n
        self.got = [0.0, 0.0]

    def hop(self, tie, *others):
        n, self.d = self.n, self.d - 1
        d = self.d
        right, left = self.parts[d] + self.got[0], self.parts[n - d] + self.got[1]
        self.got = [
            lax.ppermute(tie(right, *others), "kv", [(i, i + 1) for i in range(n - d)]),
            lax.ppermute(tie(left, *others), "kv", [(i + 1, i) for i in range(d - 1, n - 1)]),
        ]
        return self.got

    def total(self):
        return self.parts[0] + self.got[0] + self.got[1]


def in_order(blocks, z, n):
    stacked = jnp.stack(blocks)
    return jnp.concatenate(
        [lax.dynamic_index_in_dim(stacked, (j - z + n) % n, 0, keepdims=False) for j in range(n)]
    )


def exchange(blocks, n):
    got = [blocks[0]]
    for d in range(1, n):
        got.append(lax.ppermute(blocks[n - d], "kv", [((i + d) % n, i) for i in range(n)]))
    return got


def whole_kernel(thin, deep, shares_ref, in_ref, so_ref, co_ref, *refs):
    so_out, co_out, cq_out, kv_out = refs[-4:]
    d = pl.program_id(0)
    half = shares_ref.shape[3]
    qcols = cq_out.shape[2]

    @pl.when(d == 0)
    def _():
        so_out[...] = so_ref[...]
        co_out[...] = co_ref[...]
        cq_out[0] = in_ref[:, :qcols]
        kv_out[0] = in_ref[:, qcols:]

    @pl.when(d > 0)
    def _():
        for i in range(shares_ref.shape[0]):
            here = shares_ref[i, 0, 0:deep, :].astype(jnp.bfloat16)
            cq_out[0, i * deep:(i + 1) * deep, :] = here[:, :qcols]
            kv_out[0, i * deep:(i + 1) * deep, :] = here[:, qcols:]
            for n, ref in enumerate((so_out, co_out)):
                for side in range(2):
                    at = deep + (2 * n + side) * thin
                    ref[i * thin:(i + 1) * thin, side * half:(side + 1) * half] = (
                        shares_ref[i, 0, at:at + thin, :].astype(jnp.bfloat16)
                    )


def whole_weights(shares, own_in, own_so, own_co, earlier):
    nb, others = shares.shape[:2]
    width, cols = own_in.shape
    tall = own_so.shape[0]
    step = 4
    turns = nb // step
    own = lambda d, i: (jnp.where(d == 0, i, turns - 1), 0)
    flat = pl.BlockSpec((tall // turns, width), lambda d, i: (d * turns + i, 0))
    deep = pl.BlockSpec((1, width // turns, cols // 2), lambda d, i: (d, i, 0))
    return pl.pallas_call(
        functools.partial(whole_kernel, tall // nb, width // nb),
        out_shape=(jax.ShapeDtypeStruct(((others + 1) * tall, width), jnp.bfloat16),) * 2
        + (jax.ShapeDtypeStruct((others + 1, width, cols // 2), jnp.bfloat16),) * 2,
        grid=(others + 1, turns),
        in_specs=[
            pl.BlockSpec((step, 1) + shares.shape[2:], lambda d, i: (jnp.where(d == 0, 0, i), jnp.maximum(d - 1, 0), 0, 0)),
            pl.BlockSpec((width // turns, cols), own),
            pl.BlockSpec((tall // turns, width), own),
            pl.BlockSpec((tall // turns, width), own),
        ] + [pl.BlockSpec((16, 128), lambda d, i: (0, 0))] * len(earlier),
        out_specs=(flat, flat, deep, deep),
        compiler_params=pltpu.CompilerParams(dimension_semantics=("arbitrary", "arbitrary"), vmem_limit_bytes=32 << 20),
        cost_estimate=cost(shares.size, 7),
        name="whole_weights",
    )(shares, own_in, own_so, own_co, *earlier)


def on_device(
    inputs,
    memory,
    out_grad,
    gain_self,
    self_query,
    self_key,
    self_value,
    self_output,
    self_table,
    gain_cross,
    cross_query,
    cross_key,
    cross_value,
    cross_output,
    cross_table,
    gain_ffn,
    ffn_gate,
    ffn_up,
    ffn_down,
):
    seq_len = inputs.shape[1]
    width = inputs.shape[2]
    n, nb = lax.axis_size("kv"), lax.axis_size("batch")
    z, b = lax.axis_index("kv"), lax.axis_index("batch")
    rows = seq_len // n
    low = jnp.bfloat16
    one = jnp.where(gain_self[0] < 100, 1.0, 2.0).astype(jnp.float32)

    def settle(x):
        return x * one

    def tie(x, *others):
        for other in others:
            x = x + other[(0,) * other.ndim].astype(jnp.float32) * (one - 1.0)
        return x

    def share(w):
        return block_of(w, b, w.shape[0] // nb).astype(jnp.float32)

    def halves(x):
        return jnp.concatenate([x[:, :width // 2], x[:, width // 2:]])

    qcols, kcols, ocols = cross_query.shape[1], cross_key.shape[1], cross_output.shape[0]
    far_pairs = [(i, i ^ 2) for i in range(n)]
    near_pairs = [(i, i ^ 1) for i in range(n)]
    cross_kv = jnp.concatenate([cross_key, cross_value], axis=1)
    unit = jnp.concatenate(
        [
            jnp.concatenate([share(cross_query), share(cross_kv)], axis=1),
            halves(share(self_output)),
            halves(share(cross_output)),
        ]
    )
    units = exchange([unit] * n, n)[1:]

    gain_one = gain_self.astype(jnp.float32)
    gain_two = gain_cross.astype(jnp.float32)
    gain_three = gain_ffn.astype(jnp.float32)
    self_x, own_cross_x = bias_vectors(self_table, False), bias_vectors(cross_table, True)

    flat_in = inputs.reshape(seq_len, width).astype(jnp.float32)
    flat_mem = memory.reshape(memory.shape[1], width)
    attn_in = norm_rows(flat_in, gain_one).astype(low)
    zero = jnp.zeros((1,), jnp.int32)
    self_kv = jnp.concatenate([self_key, self_value], axis=1)
    sq = mm(self_query, attn_in, T0).astype(low)
    skv = mm(self_kv, attn_in, T0).astype(low)
    mixed, self_log = attend(zero, self_x, sq, skv, True)
    buckets, heads = self_table.shape
    deep, thin = width // nb, ocols // nb
    shares = lax.all_gather(tie(jnp.stack(units), mixed), "batch")
    mixed = tie(mixed.astype(jnp.float32), *units)
    rider = own_cross_x.reshape(-1, rows)
    own_self = jnp.concatenate([self_query, self_kv], axis=1)
    got = exchange([jnp.concatenate([block_of(mixed, (z + d) % n, rows, 1), rider]) for d in range(n)], n)
    others = got[1:]
    mixed_self = settle(jnp.concatenate([x[:ocols] for x in got])).astype(low)
    ridden = ocols + rider.shape[0]
    cross_x = jnp.concatenate([x[ocols:ridden] for x in got]).reshape(-1, 8, rows)
    own_in = jnp.concatenate([cross_query, cross_kv], axis=1)
    whole_so, whole_co, whole_cq, whole_kv = whole_weights(
        shares, own_in, self_output, cross_output, [mixed_self, cross_x.reshape(-1, rows)]
    )

    sent = jnp.stack([share(ffn_gate.T), share(ffn_up.T), share(ffn_down)])
    fetched = lax.ppermute(tie(sent, *others), "kv", far_pairs)
    sent = lax.all_gather(tie(fetched, whole_so), "batch", axis=1, tiled=True)

    in_rows = block_of(inputs.reshape(seq_len, width), z, rows).astype(jnp.float32)
    after_self = in_rows + mm(mixed_self, whole_so, TN)

    def into(w, x):
        y = lax.dot_general(w, x, (((1,), (1,)), ((), ())), preferred_element_type=jnp.float32)
        return y.astype(low).reshape(-1, x.shape[0])

    ckv = into(whole_kv, flat_mem)
    cross_in = norm_rows(after_self, gain_two).astype(low)
    cq = into(whole_cq, cross_in)
    place = z.reshape(1).astype(jnp.int32) * (rows // QB)
    mixed_cross, cross_log = attend(place, cross_x, cq, ckv, False)
    after_cross = after_self + mm(mixed_cross, whole_co, TN)

    ffn_in = norm_rows(after_cross, gain_three).astype(low)
    other = settle(lax.ppermute(ffn_in.astype(jnp.float32), "kv", near_pairs)).astype(low)
    flat_grad = out_grad.reshape(seq_len, width)
    own_grad = block_of(flat_grad, z, rows)
    far_ffn = settle(sent).astype(low)
    weights = ((ffn_gate, ffn_up, ffn_down, False), (far_ffn[0], far_ffn[1], far_ffn[2], True))
    parts, grads, inputs_of = [], [], ((ffn_in, own_grad), (other, block_of(flat_grad, z ^ 1, rows)))
    for x, dy in inputs_of:
        in_part = out_part = 0.0
        for w_gate, w_up, w_down, turned in weights:
            there, back = (NT, NN) if turned else (NN, NT)
            gate_pre, up_pre = mm(x, w_gate, there), mm(x, w_up, there)
            hidden = gate_times_up(gate_pre, up_pre).astype(low)
            out_part = out_part + mm(hidden, w_down, NN)
            gate_grad, up_grad = jax.vjp(gate_times_up, gate_pre, up_pre)[1](mm(dy, w_down, NT))
            gate_grad, up_grad = gate_grad.astype(low), up_grad.astype(low)
            in_part = in_part + mm(gate_grad, w_gate, back) + mm(up_grad, w_up, back)
            grads.append((gate_grad, up_grad, hidden))
        parts.append((in_part, out_part))
    ffn_in_grad = parts[0][0] + lax.ppermute(parts[1][0], "kv", near_pairs)
    both_in, both_grad = (jnp.concatenate(x) for x in zip(*inputs_of))
    ffn_sums = jnp.stack(
        [
            mm(jnp.concatenate([grads[side][kind], grads[2 + side][kind]]), both_grad if kind == 2 else both_in, TN)
            for side in range(2) for kind in range(3)
        ]
    )
    ffn_sums = lax.psum_scatter(ffn_sums, "batch", scatter_dimension=1, tiled=True)
    ffn_out = parts[0][1] + lax.ppermute(tie(parts[1][1], ffn_in_grad), "kv", near_pairs)

    norm_grad, grad_gain_ffn = jax.vjp(norm_rows, after_cross, gain_three)[1](ffn_in_grad)
    cross_out_grad = own_grad.astype(jnp.float32) + norm_grad
    branch_cross = cross_out_grad.astype(low)
    mixed_grad = mm(whole_co, branch_cross, NT).astype(low)
    cq_grad, ckv_grad, cross_lines = attend_back(
        place, cross_x, cq, ckv, mixed_grad, cross_log, False
    )
    cross_in_grad = lax.dot_general(
        cq_grad.reshape(n, qcols, rows), whole_cq, (((0, 1), (0, 2)), ((), ())), preferred_element_type=jnp.float32
    )
    norm_grad, grad_gain_cross = jax.vjp(norm_rows, after_self, gain_two)[1](cross_in_grad)
    self_out_grad = cross_out_grad + norm_grad
    branch_self = self_out_grad.astype(low)
    mixed_grad = tie(mm(whole_so, branch_self, NT).astype(low).astype(jnp.float32), ffn_out)
    got = exchange([mixed_grad[d * ocols:(d + 1) * ocols] for d in range(n)], n)
    arrived = got[1:]
    stacked = jnp.stack(got)
    mixed_grad = tie(
        jnp.concatenate(
            [lax.dynamic_index_in_dim(stacked, (j - z + n) % n, 0, keepdims=False) for j in range(n)], axis=1
        ),
    )
    mixed_grad = settle(mixed_grad).astype(low)
    memory_part = lax.dot_general(
        ckv_grad.reshape(n, 2 * kcols, -1), whole_kv, (((0, 1), (0, 2)), ((), ())), preferred_element_type=jnp.float32
    )
    memory_grad = lax.psum_scatter(tie(memory_part, *arrived), "kv", scatter_dimension=1, tiled=True)

    arriving = exchange([tie(share(own_self), fetched, after_cross)] * n, n)[1:]
    rest_self = tie(jnp.stack(arriving), cq_grad, ffn_sums)
    rest_self = settle(lax.all_gather(rest_self, "batch", axis=1, tiled=True)).astype(low)

    sq_grad, skv_grad, self_lines = attend_back(zero, self_x, sq, skv, mixed_grad, self_log, True)
    turned = jnp.concatenate([sq_grad, skv_grad]).astype(jnp.float32)
    got = exchange([block_of(turned, (z + d) % n, rows, 1) for d in range(n)], n)
    rest = settle(jnp.stack(got[1:])).astype(low)
    attn_in_grad = mm(got[0].astype(low), own_self, T0) + lax.dot_general(
        rest, rest_self, (((0, 1), (0, 2)), ((), ())), preferred_element_type=jnp.float32
    )
    early = got[1:]
    attn_term = mm(sq_grad, self_query, T0) + mm(skv_grad, self_kv, T0)
    norm_grad, _ = jax.vjp(norm_rows, in_rows, gain_one)[1](attn_in_grad)
    last = self_out_grad + norm_grad
    _, grad_gain_self = jax.vjp(norm_rows, flat_in, gain_one)[1](attn_term)

    result = (tie(after_cross, *early) + ffn_out).astype(low).astype(jnp.float32)
    line = Gather(result, n)
    ends_line = Gather(last, n)
    one_hop = ends_line.hop(tie)
    two_hops = ends_line.hop(tie)
    three_hops = ends_line.hop(tie)
    line.hop(tie)
    lo_two = line.hop(tie)
    line.hop(tie)
    layer_out = settle(in_order(line.blocks(), z, n)).astype(low)
    input_grad = in_order(ends_line.blocks(), z, n)

    self_tab = table_gradient(self_lines, False, buckets)
    cross_tab = table_gradient(cross_lines, True, buckets)
    spots = [(z + d) % n for d in range(n)]
    tabs = jnp.zeros((2, n, buckets * heads), jnp.float32)
    tabs = lax.dynamic_update_slice(tabs, self_tab.reshape(1, 1, -1), (0, z, 0))
    for d in range(n):
        tabs = lax.dynamic_update_slice(
            tabs, cross_tab[:, d * heads:(d + 1) * heads].reshape(1, 1, -1), (1, spots[d], 0)
        )
    small = jnp.stack([grad_gain_self, grad_gain_cross, grad_gain_ffn, jnp.pad(tabs.reshape(-1), (0, width - tabs.size))], axis=1)
    small = jnp.pad(tie(small, *early), ((0, 0), (0, 124)))
    sums = jnp.concatenate(
        [
            mm(branch_cross, mixed_cross, T0),
            mm(cross_in, cq_grad, T0),
            mm(flat_mem, ckv_grad, T0),
            mm(branch_self, mixed_self, T0),
            mm(attn_in, sq_grad, T0),
            mm(attn_in, skv_grad, T0),
            small,
        ],
        axis=1,
    )
    sums = lax.psum_scatter(sums, "batch", tiled=True)
    self_sums, small = sums[:, 4 * width:-128], sums[:, -128:]
    parts = [
        jnp.concatenate(
            [sums[:, at * width + d * size:at * width + (d + 1) * size]
             for at, size in enumerate((ocols, qcols, 2 * kcols, ocols))] + [small],
            axis=1,
        )
        for d in range(n)
    ]
    attn_sums = sum(exchange([tie(x, *three_hops) for x in parts], n))
    ffn_sums = ffn_sums[:3] + lax.ppermute(tie(ffn_sums[3:], *arrived), "kv", far_pairs)
    ffn_sums = lax.all_gather(tie(ffn_sums, last, memory_grad), "batch", axis=1, tiled=True)
    attn_sums = lax.all_gather(tie(jnp.concatenate([attn_sums, self_sums], axis=1), *lo_two), "batch", tiled=True)

    def columns(x, sizes):
        at = 0
        for size in sizes:
            yield x[:, at:at + size]
            at += size

    grad_co, grad_cq, grad_ck, grad_cv, grad_so, small, grad_sq, grad_sk, grad_sv = columns(
        attn_sums,
        (ocols, qcols, kcols, kcols, ocols, 128, self_query.shape[1], self_key.shape[1], self_value.shape[1]),
    )
    small = small[:, :4].T
    tabs = small[3, :tabs.size].reshape(tabs.shape)
    tabs = lax.dynamic_index_in_dim(tabs, z, 1, keepdims=False).reshape(2, buckets, heads)
    return (
        layer_out.reshape(inputs.shape),
        input_grad.reshape(inputs.shape),
        memory_grad.reshape(1, memory.shape[1], width // n),
        small[0],
        grad_sq,
        grad_sk,
        grad_sv,
        grad_so.T,
        tabs[0],
        small[1],
        grad_cq,
        grad_ck,
        grad_cv,
        grad_co.T,
        tabs[1],
        small[2],
        ffn_sums[0].T,
        ffn_sums[1].T,
        ffn_sums[2],
    )


def solution(mesh):
    return jax.shard_map(
        on_device,
        mesh=mesh,
        in_specs=(
            P("batch", None, None),
            P("batch", None, None),
            P("batch", None, None),
            P(),
            P(None, "kv"),
            P(None, "kv"),
            P(None, "kv"),
            P("kv", None),
            P(None, "kv"),
            P(),
            P(None, "kv"),
            P(None, "kv"),
            P(None, "kv"),
            P("kv", None),
            P(None, "kv"),
            P(),
            P(None, "kv"),
            P(None, "kv"),
            P("kv", None),
        ),
        out_specs=(
            P("batch", None, None),
            P("batch", None, None),
            P("batch", None, "kv"),
            P(),
            P(None, "kv"),
            P(None, "kv"),
            P(None, "kv"),
            P("kv", None),
            P(None, "kv"),
            P(),
            P(None, "kv"),
            P(None, "kv"),
            P(None, "kv"),
            P("kv", None),
            P(None, "kv"),
            P(),
            P(None, "kv"),
            P(None, "kv"),
            P("kv", None),
        ),
        check_vma=False,
    )
```
